512 devices in a mesh: row: 32 (over z, x_hi), col: 16 (over x_lo, y, core).
Axes of the slice: x: 4 (x_hi: 2, x_lo: 2; x = x_hi * 2 + x_lo), y: 4, z: 16, core: 2. Of those that a mesh axis runs over, the one named last changes fastest.
Arguments:
- inverse_set: float32 [1, 32, 128, 2, 16, 128], P(None, 'row', None, None, 'col'), may hold values from -6 to 6
- presence: int32 [1, 32, 2, 16], P(None, 'row', None, 'col'), may hold values 0 or 1
- factor: float32 [1, 32, 128, 512], P(None, 'row'), may hold values from -0.09375 to 0.09375
- dinv: float32 [512, 512], P('row', 'col'), may hold values from -6 to 6
Outputs:
- off_diag: float32 [1, 32, 128, 512], P(None, 'row', 'col')
- diag_block: float32 [512, 512], P('row', 'col')
The draws below stay inside these ranges and needn't reach their ends.
All inputs are finite; a program needn't handle non-finite values. No bound on the sum of `presence` on one device may be relied on, other than what follows from the above.
Results may differ from the reference program's by a relative error of at most 0.00007.
Values sent between devices are 32-bit elements; how exact they have to be, the bound alone decides.
A program may use at most 64 MiB of HBM per device.

```python
import jax
import jax.numpy as jnp
from jax import lax

BR = 1
BS = 128
GR = 32
GC = 16
BC = 2
ORDER = 4096
PW = 512


def touch_ends(entries, own_key, least, largest):
    longest = entries.shape.index(max(entries.shape))
    spots = []
    for shift in (0, 1):
        where = [jax.random.randint(jax.random.fold_in(own_key, axis), (), 0, length) for axis, length in enumerate(entries.shape)]
        where[longest] = (where[longest] + shift) % entries.shape[longest]
        spots.append(tuple(where))
    return entries.at[spots[0]].set(least).at[spots[1]].set(largest)


def block_scale(own_key, shape, split, low, high):
    gain, own = 1.0, jax.random.fold_in(own_key, 6)
    for axis_at, shards_of in split:
        draws = jnp.exp(jax.random.uniform(jax.random.fold_in(own, axis_at), (shards_of,), jnp.float32, low / len(split), high / len(split)))
        gain = gain * jnp.repeat(draws, shape[axis_at] // shards_of).reshape([-1 if axis == axis_at else 1 for axis in range(len(shape))])
    return gain


def bell_draw(key, extent, spread, bound, cuts=(), held_as=jnp.bfloat16):
    entries = spread * jax.random.normal(key, extent, jnp.float32)
    if cuts:
        entries = entries * block_scale(key, extent, cuts, -0.22, 0.18)
    return jnp.clip(entries, -bound, bound).astype(held_as)


def setup_inputs(seed: int = 0) -> dict:
    streams_of = jax.random.split(jax.random.key(seed), 5)
    inverse_set = bell_draw(streams_of[0], (BR, GR, BS, BC, GC, BS), 1.0, 6.0, ((1, 32), (4, 16)), jnp.float32)
    presence = touch_ends((jax.random.randint(streams_of[1], (BR, GR, BC, GC), 0, 20) < 17).astype(jnp.int32), jax.random.fold_in(streams_of[1], 1), 0, 1)
    factor = bell_draw(streams_of[2], (BR, GR, BS, PW), ORDER ** -0.5, 0.09375, ((1, 32),), jnp.float32)
    dinv = bell_draw(streams_of[3], (PW, PW), 1.0, 6.0, ((0, 32), (1, 16)), jnp.float32)
    return dict(inverse_set=inverse_set, presence=presence, factor=factor, dinv=dinv)


def reference(inverse_set, presence, factor, dinv):
    flat = factor.reshape(BR * GR * BS, PW)
    weights = presence.astype(inverse_set.dtype)

    def one_row(args):
        blocks, marks = args
        masked = blocks * marks[:, None, :, :, None]
        return jnp.dot(masked.reshape(GR * BS, BR * GR * BS), flat, precision=lax.Precision.HIGHEST, preferred_element_type=jnp.float32)

    update = lax.map(one_row, (inverse_set, weights))
    update = update.reshape(BR, GR, BS, PW)
    off_diag = -update
    diag_block = dinv + jnp.dot(flat.T, update.reshape(BR * GR * BS, PW), precision=lax.Precision.HIGHEST, preferred_element_type=jnp.float32)
    return (off_diag, diag_block)
```

```python
import jax
import jax.numpy as jnp
from jax import lax
from jax.experimental import pallas as pl
from jax.experimental.pallas import tpu as pltpu
from jax.sharding import PartitionSpec as P

MESH = pl.DeviceIdType.MESH
NROW = 32
NCOL = 16
F32 = jnp.float32
BF16 = jnp.bfloat16
NT = (((1,), (1,)), ((), ()))


def split(value):
    high = value.astype(BF16)
    return high, (value - high.astype(F32)).astype(BF16)


def dot_nt(a, b):
    return lax.dot_general(a, b, NT, preferred_element_type=F32)


def kernel(
    inv_hbm, pres_ref, fac_hbm, off_ref, diag_ref,
    a_raw, f_raw, ft, abuf, fbuf, pad, q, trecv, vbuf, vrecv,
    load_sem, f_send, f_recv, b_recv, a_send, a_recv, core_recv, t_send, t_recv, v_send, v_recv,
):
    r = lax.axis_index("row")
    c = lax.axis_index("col")
    xh = lax.rem(r, 2)
    core = lax.rem(c, 2)
    y = lax.rem(lax.div(c, 2), 4)
    xl = lax.div(c, 8)

    load_f = pltpu.make_async_copy(fac_hbm, f_raw, load_sem.at[0])
    load_a = pltpu.make_async_copy(inv_hbm, a_raw, load_sem.at[1])
    load_f.start()
    load_a.start()

    def other(col):
        return lax.rem(col + 8, NCOL)

    r_pair = r + 1 - 2 * xh
    c_x = other(c)
    c_up = xl * 8 + lax.rem(y + 1, 4) * 2 + core
    c_down = xl * 8 + lax.rem(y + 3, 4) * 2 + core
    c_far = xl * 8 + lax.rem(y + 2, 4) * 2 + core
    c_core = c + 1 - 2 * core

    z_up = (lax.rem(r + 2, NROW), c)
    z_down = (lax.rem(r + 30, NROW), c)
    cross = (r_pair, c_x)
    x_pair = (r, c_x)
    y_up = (r, c_up)
    y_down = (r, c_down)
    twin = (r, c_core)

    barrier = pltpu.get_barrier_semaphore()
    for peer in (z_up, z_down, cross, x_pair, y_up, y_down, twin):
        pl.semaphore_signal(barrier, inc=1, device_id=peer, device_id_type=MESH)

    pad[...] = jnp.zeros_like(pad)

    load_f.wait()
    for part in range(4):
        ft[128 * part : 128 * (part + 1), :] = f_raw[:, 128 * part : 128 * (part + 1)].T
    own_rows = pl.multiple_of(32 * c, 32)
    cross_rows = pl.multiple_of(32 * c_x, 32)
    fbuf[r] = ft[pl.ds(own_rows, 32), :]

    load_a.wait()
    for b in range(2):
        abuf[c, b] = a_raw[pl.ds(b, 128, stride=2), :] * pres_ref[0, b].astype(F32)

    pl.semaphore_wait(barrier, 7)

    def send(src, dst, send_sem, recv_sem, peer):
        pltpu.make_async_remote_copy(
            src_ref=src, dst_ref=dst, send_sem=send_sem, recv_sem=recv_sem,
            device_id=peer, device_id_type=MESH,
        ).start()

    def wait(ref, sem):
        pltpu.make_async_copy(ref, ref, sem).wait()

    bases = (r, r_pair)

    def slot(way, chunk, dist):
        step = -2 * dist if way == 0 else 2 * dist
        return lax.rem(bases[chunk] + step + NROW, NROW)

    def reach(way, chunk):
        return 8 if way == chunk else 7

    def pass_on(way, chunk, dist):
        if dist > reach(way, chunk):
            return
        at = slot(way, chunk, dist - 1)
        src = ft.at[pl.ds(own_rows, 32), :] if dist == 1 and chunk == 0 else fbuf.at[at]
        send(src, fbuf.at[at], f_send, f_recv.at[way, chunk, dist - 1], z_up if way == 0 else z_down)

    def take(way, chunk, dist):
        if dist > reach(way, chunk):
            return
        wait(fbuf.at[slot(way, chunk, dist)], f_recv.at[way, chunk, dist - 1])
        pass_on(way, chunk, dist + 1)

    def give(col, b, peer, sem):
        send(abuf.at[col, b], abuf.at[col, b], a_send, sem, peer)

    def got(col, b, sem):
        wait(abuf.at[col, b], a_recv.at[sem])

    pass_on(0, 0, 1)
    pass_on(1, 0, 1)
    send(ft.at[pl.ds(cross_rows, 32), :], fbuf.at[r], f_send, b_recv, cross)
    for b in range(2):
        give(c, b, y_up, a_recv.at[b])
        give(c, b, y_down, a_recv.at[2 + b])
        give(c, b, x_pair, a_recv.at[4 + b])
        give(c, b, twin, core_recv)

    def near_y(b):
        got(c_down, b, b)
        if b == 0:
            give(c_down, b, y_up, a_recv.at[6])
        give(c_down, b, twin, core_recv)
        got(c_up, b, 2 + b)
        if b == 1:
            give(c_up, b, y_down, a_recv.at[7])
        give(c_up, b, twin, core_recv)

    def near_x(b):
        got(c_x, b, 4 + b)
        give(c_x, b, y_up, a_recv.at[8 + b])
        give(c_x, b, y_down, a_recv.at[10 + b])
        give(c_x, b, twin, core_recv)

    def far_y(b):
        got(c_far, b, 6 + b)
        give(c_far, b, x_pair, a_recv.at[12 + b])
        give(c_far, b, twin, core_recv)

    def diagonal(b):
        got(other(c_down), b, 8 + b)
        give(other(c_down), b, twin, core_recv)
        got(other(c_up), b, 10 + b)
        give(other(c_up), b, twin, core_recv)

    def farthest(b):
        got(other(c_far), b, 12 + b)
        give(other(c_far), b, twin, core_recv)

    def both(chunk, dist):
        take(0, chunk, dist)
        take(1, chunk, dist)

    wait(fbuf.at[r_pair], b_recv)
    pass_on(0, 1, 1)
    pass_on(1, 1, 1)
    both(0, 1)
    near_y(0)
    near_x(0)
    both(1, 1)
    both(0, 2)
    near_y(1)
    near_x(1)
    both(1, 2)
    both(0, 3)
    far_y(0)
    far_y(1)
    both(1, 3)
    both(0, 4)
    diagonal(0)
    both(1, 4)
    both(0, 5)
    diagonal(1)
    both(1, 5)
    both(0, 6)
    farthest(0)
    farthest(1)
    both(1, 6)
    both(0, 7)
    both(1, 7)
    wait(abuf.at[pl.ds(0, 8)], core_recv)

    def block(total, at):
        high, low = split(fbuf[at])
        a_high, a_low = split(abuf[lax.rem(at, NCOL), lax.div(at, NCOL)])
        first = dot_nt(jnp.concatenate([high, low], axis=0), a_high)
        return total + (first[:32] + first[32:]) + dot_nt(high, a_low)

    def near(dist, total):
        for chunk in range(2):
            total = block(total, lax.rem(bases[chunk] + 2 * dist, NROW))
            total = block(total, lax.rem(bases[chunk] - 2 * dist + NROW, NROW))
        return total

    total = jnp.zeros((32, 128), F32)
    for chunk in range(2):
        total = block(total, bases[chunk])
    total = lax.fori_loop(1, 8, near, total)
    for chunk in range(2):
        take(chunk, chunk, 8)
        total = block(total, slot(chunk, chunk, 8))

    t_high, t_low = split(total)
    packed = jnp.zeros((128, 128), F32)
    for g in range(4):
        high, low = split(ft[pl.ds(g, 128, stride=4), :])
        parts = []
        for half in (t_high, t_low):
            zero = jnp.zeros((32, 128), BF16)
            parts.append(jnp.concatenate([half if g == at else zero for at in range(4)], axis=0))
        first = dot_nt(jnp.concatenate([high, low], axis=0), parts[0])
        packed = packed + (first[:128] + first[128:]) + dot_nt(high, parts[1])
    for at in range(NROW):
        q[at] = packed[4 * at : 4 * at + 4, :]
    far_first = sorted(range(1, NROW), key=lambda step: -min(step // 2, 16 - step // 2))
    for step in far_first:
        goal = lax.rem(r + step, NROW)
        send(q.at[goal], trecv.at[step - 1], t_send, t_recv, (goal, c))

    pad[pl.ds(pl.multiple_of(32 * lax.rem(c, 4), 32), 32), :] = total
    vbuf[...] = pad[...].T
    vrecv[c] = vbuf[pl.ds(pl.multiple_of(8 * c, 8), 8), :]
    for step in range(1, NCOL):
        goal = lax.rem(c + step, NCOL)
        send(vbuf.at[pl.ds(pl.multiple_of(8 * goal, 8), 8), :], vrecv.at[c], v_send, v_recv, (r, goal))

    wait(vrecv.at[pl.ds(0, NCOL - 1)], v_recv)
    for g in range(4):
        rows = vrecv[4 * g] + vrecv[4 * g + 1] + vrecv[4 * g + 2] + vrecv[4 * g + 3]
        off_ref[:, 128 * g : 128 * (g + 1)] = rows

    wait(trecv, t_recv)
    tile = q[r]
    for step in range(NROW - 1):
        tile = tile + trecv[step]
    for g in range(4):
        diag_ref[pl.ds(g, 4, stride=4), :] = tile[:, 32 * g : 32 * (g + 1)]

    wait(fbuf.at[pl.ds(0, 31)], f_send)
    wait(abuf.at[pl.ds(0, 15)], a_send)
    wait(q.at[pl.ds(0, 31)], t_send)
    wait(vrecv.at[pl.ds(0, NCOL - 1)], v_send)


def local(inverse_set, presence, factor, dinv):
    update, diag_sum = pl.pallas_call(
        kernel,
        out_shape=(jax.ShapeDtypeStruct((8, 512), F32), jax.ShapeDtypeStruct((16, 32), F32)),
        in_specs=[
            pl.BlockSpec(memory_space=pl.ANY),
            pl.BlockSpec(memory_space=pltpu.SMEM),
            pl.BlockSpec(memory_space=pl.ANY),
        ],
        out_specs=(pl.BlockSpec(memory_space=pltpu.VMEM), pl.BlockSpec(memory_space=pltpu.VMEM)),
        scratch_shapes=[
            pltpu.VMEM((256, 128), F32),
            pltpu.VMEM((128, 512), F32),
            pltpu.VMEM((512, 128), F32),
            pltpu.VMEM((NCOL, 2, 128, 128), F32),
            pltpu.VMEM((NROW, 32, 128), F32),
            pltpu.VMEM((128, 128), F32),
            pltpu.VMEM((NROW, 4, 128), F32),
            pltpu.VMEM((NROW - 1, 4, 128), F32),
            pltpu.VMEM((128, 128), F32),
            pltpu.VMEM((NCOL, 8, 128), F32),
            pltpu.SemaphoreType.DMA((2,)),
            pltpu.SemaphoreType.DMA,
            pltpu.SemaphoreType.DMA((2, 2, 8)),
            pltpu.SemaphoreType.DMA,
            pltpu.SemaphoreType.DMA,
            pltpu.SemaphoreType.DMA((14,)),
            pltpu.SemaphoreType.DMA,
            pltpu.SemaphoreType.DMA,
            pltpu.SemaphoreType.DMA,
            pltpu.SemaphoreType.DMA,
            pltpu.SemaphoreType.DMA,
        ],
        compiler_params=pltpu.CompilerParams(collective_id=0, has_side_effects=True),
    )(
        inverse_set.reshape(256, 128),
        presence.reshape(1, 2),
        factor.reshape(128, 512),
    )
    return (-update).reshape(1, 1, 8, 512), dinv + diag_sum


def solution(mesh):
    in_specs = (
        P(None, "row", None, None, "col", None),
        P(None, "row", None, "col"),
        P(None, "row", None, None),
        P("row", "col"),
    )
    out_specs = (P(None, "row", "col", None), P("row", "col"))
    return jax.shard_map(local, mesh=mesh, in_specs=in_specs, out_specs=out_specs, check_vma=False)
```

```python
import jax
import jax.numpy as jnp
from jax import lax
from jax.experimental import pallas as pl
from jax.experimental.pallas import tpu as pltpu
from jax.sharding import PartitionSpec as P

MESH = pl.DeviceIdType.MESH
NROW = 32
NCOL = 16
F32 = jnp.float32
BF16 = jnp.bfloat16
NT = (((1,), (1,)), ((), ()))
JUMP = 5
PLANE = [(dx, dy) for dx in range(2) for dy in range(4)]


def split(value):
    high = value.astype(BF16)
    return high, (value - high.astype(F32)).astype(BF16)


def dot_nt(a, b):
    return lax.dot_general(a, b, NT, preferred_element_type=F32)


def kernel(
    inv_hbm, pres_ref, fac_hbm, off_ref, diag_ref,
    a_raw, f_raw, ft, abuf, fbuf, fsplit, ftsplit, pad, q, trecv, vbuf, vrecv, mate, drecv,
    load_sem, f_send, f_first, f_rest, a_send, a_even, a_odd, t_send, t_recv, v_send, v_recv, d_send, d_recv,
):
    r = lax.axis_index("row")
    c = lax.axis_index("col")
    xh = lax.rem(r, 2)
    core = lax.rem(c, 2)
    y = lax.rem(lax.div(c, 2), 4)
    xl = lax.div(c, 8)
    chip = lax.div(c, 2)
    r_pair = r + 1 - 2 * xh
    c_cross = lax.rem(c + 8, NCOL)

    load_a = pltpu.make_async_copy(inv_hbm, a_raw, load_sem.at[0])
    load_f = pltpu.make_async_copy(fac_hbm, f_raw, load_sem.at[1])

    def send(src, dst, send_sem, recv_sem, peer):
        pltpu.make_async_remote_copy(
            src_ref=src, dst_ref=dst, send_sem=send_sem, recv_sem=recv_sem,
            device_id=peer, device_id_type=MESH,
        ).start()

    def wait(ref, sem):
        pltpu.make_async_copy(ref, ref, sem).wait()

    def at_plane(dx, dy, of_core):
        return lax.rem(xl + dx, 2) * 8 + lax.rem(y + dy, 4) * 2 + of_core

    def row_off(base, dz):
        return lax.rem(base + 2 * dz + NROW, NROW)

    def mask_own():
        load_a.wait()
        for b in range(2):
            abuf[c, b] = a_raw[pl.ds(b, 128, stride=2), :] * pres_ref[0, b].astype(F32)

    barrier = pltpu.get_barrier_semaphore()

    def greet(peer):
        pl.semaphore_signal(barrier, inc=1, device_id=peer, device_id_type=MESH)

    def put_update():
        for h in range(4):
            off_ref[:, 128 * h : 128 * (h + 1)] = vrecv[2 * h] + vrecv[2 * h + 1]

    @pl.when(core == 1)
    def _():
        load_a.start()
        mask_own()
        pl.semaphore_wait(barrier, 8)
        for dx, dy in reversed(PLANE):
            there = dx * 4 + (4 - dy) % 4
            send(abuf.at[c], abuf.at[c], a_send, a_odd.at[there], (r, at_plane(dx, dy, 0)))
        wait(vrecv, v_recv)
        put_update()
        wait(drecv, d_recv)
        diag_ref[...] = drecv[...]
        wait(abuf.at[pl.ds(0, 8)], a_send)

    @pl.when(core == 0)
    def _():
        load_f.start()
        load_a.start()
        for dx, dy in PLANE:
            greet((r, at_plane(dx, dy, 1)))
            if (dx, dy) != (0, 0):
                greet((r, at_plane(dx, dy, 0)))
        for dz in (5, 3, 2, 1):
            greet((row_off(r, dz), c))
            greet((row_off(r, -dz), c))
        for dz in (5, 2, 1):
            greet((row_off(r_pair, dz), c_cross))
            greet((row_off(r_pair, -dz), c_cross))
        greet((r_pair, c_cross))

        load_f.wait()
        for part in range(4):
            ft[128 * part : 128 * (part + 1), :] = f_raw[:, 128 * part : 128 * (part + 1)].T
        own_rows = pl.ds(pl.multiple_of(32 * c, 64), 64)
        cross_rows = pl.ds(pl.multiple_of(32 * c_cross, 64), 64)
        fbuf[r] = ft[own_rows, :]
        mask_own()
        pl.semaphore_wait(barrier, 22)

        def seed(dz, first):
            if dz:
                send(ft.at[own_rows, :], fbuf.at[r], f_send, first[0], (row_off(r, dz), c))
            send(ft.at[cross_rows, :], fbuf.at[r], f_send, first[1], (row_off(r_pair, dz), c_cross))

        seed(JUMP, (f_first.at[0, 0], f_first.at[0, 1]))
        seed(-JUMP, (f_first.at[1, 0], f_first.at[1, 1]))
        for dx, dy in reversed(PLANE[1:]):
            send(abuf.at[c], abuf.at[c], a_send, a_even, (r, at_plane(dx, dy, 0)))
        for dz in (2, -2, 1, -1, 0):
            seed(dz, (f_rest, f_rest))

        for g in range(2):
            high, low = split(ft[pl.ds(g, 256, stride=2), :])
            ftsplit[0:256, 128 * g : 128 * (g + 1)] = high
            ftsplit[256:512, 128 * g : 128 * (g + 1)] = low
        pad[...] = jnp.zeros_like(pad)

        bases = (r, r_pair)
        for chunk in range(2):
            for way in range(2):
                sign = 1 - 2 * way
                at = row_off(bases[chunk], -sign * JUMP)
                wait(fbuf.at[at], f_first.at[way, chunk])
                steps = [3 * sign] if way == chunk else []
                for dz in steps + [2 * sign, -2 * sign, sign, -sign]:
                    send(fbuf.at[at], fbuf.at[at], f_send, f_rest, (row_off(r, dz), c))

        wait(abuf.at[pl.ds(0, 7)], a_even)
        wait(fbuf.at[pl.ds(0, 27)], f_rest)

        def lay(at, carry):
            high, low = split(fbuf[at])
            place = (lax.rem(at, 2) * 8 + lax.div(lax.rem(at, NCOL), 2)) * 2 + lax.div(at, NCOL)
            lanes = pl.ds(pl.multiple_of(128 * place, 128), 128)
            fsplit[0:64, lanes] = high
            fsplit[64:128, lanes] = low
            return carry

        lax.fori_loop(0, NROW, lay, 0)

        def product(total, dx, dy, of_core):
            col = at_plane(dx, dy, of_core)
            both = jnp.concatenate([abuf[col, 0], abuf[col, 1]], axis=1)
            rhs = jnp.concatenate(split(both), axis=0)
            lanes = pl.ds(pl.multiple_of((of_core * 8 + lax.div(col, 2)) * 256, 256), 256)
            return total + dot_nt(fsplit[:, lanes], rhs)

        total = jnp.zeros((128, 256), F32)
        for dx, dy in PLANE:
            total = product(total, dx, dy, 0)
        for dx, dy in ((0, 0), (1, 0), (0, 1), (0, 3), (1, 1), (1, 3), (0, 2), (1, 2)):
            wait(abuf.at[0], a_odd.at[dx * 4 + dy])
            total = product(total, dx, dy, 1)
        part = total[:64, :128] + (total[:64, 128:] + total[64:, :128])

        high, low = split(part)
        zero = jnp.zeros((64, 128), BF16)
        rhs = jnp.concatenate(
            [
                jnp.concatenate([high, zero, low, zero], axis=0),
                jnp.concatenate([zero, high, zero, low], axis=0),
            ],
            axis=1,
        )
        full = dot_nt(ftsplit[...], rhs)
        q[...] = (full[:256, :128] + (full[:256, 128:] + full[256:, :128])).reshape(NROW, 8, 128)
        far_first = sorted(range(1, NROW), key=lambda step: -min(step // 2, 16 - step // 2))
        for step in far_first:
            goal = lax.rem(r + step, NROW)
            send(q.at[goal], trecv.at[step - 1], t_send, t_recv, (goal, c))

        pad[pl.ds(pl.multiple_of(64 * lax.rem(chip, 2), 64), 64), :] = part
        vbuf[...] = pad[...].T
        vrecv[chip] = vbuf[pl.ds(pl.multiple_of(8 * c, 8), 8), :]
        for dx, dy in reversed(PLANE):
            for of_core in range(2):
                if (dx, dy, of_core) != (0, 0, 0):
                    col = at_plane(dx, dy, of_core)
                    rows = pl.ds(pl.multiple_of(8 * col, 8), 8)
                    send(vbuf.at[rows, :], vrecv.at[chip], v_send, v_recv, (r, col))

        wait(vrecv.at[pl.ds(0, 7)], v_recv)
        put_update()

        wait(trecv, t_recv)
        tile = q[r]
        for step in range(NROW - 1):
            tile = tile + trecv[step]
        for g in range(2):
            mate[pl.ds(g, 8, stride=2), :] = tile[:, 64 * g + 32 : 64 * g + 64]
            diag_ref[pl.ds(g, 8, stride=2), :] = tile[:, 64 * g : 64 * g + 32]
        send(mate, drecv, d_send, d_recv, (r, c + 1))

        wait(fbuf.at[pl.ds(0, 31)], f_send)
        wait(abuf.at[pl.ds(0, 7)], a_send)
        wait(q.at[pl.ds(0, 31)], t_send)
        wait(vbuf.at[pl.ds(0, 120), :], v_send)
        wait(mate, d_send)


def local(inverse_set, presence, factor, dinv):
    update, diag_sum = pl.pallas_call(
        kernel,
        out_shape=(jax.ShapeDtypeStruct((8, 512), F32), jax.ShapeDtypeStruct((16, 32), F32)),
        in_specs=[
            pl.BlockSpec(memory_space=pl.ANY),
            pl.BlockSpec(memory_space=pltpu.SMEM),
            pl.BlockSpec(memory_space=pl.ANY),
        ],
        out_specs=(pl.BlockSpec(memory_space=pltpu.VMEM), pl.BlockSpec(memory_space=pltpu.VMEM)),
        scratch_shapes=[
            pltpu.VMEM((256, 128), F32),
            pltpu.VMEM((128, 512), F32),
            pltpu.VMEM((512, 128), F32),
            pltpu.VMEM((NCOL, 2, 128, 128), F32),
            pltpu.VMEM((NROW, 64, 128), F32),
            pltpu.VMEM((128, 4096), BF16),
            pltpu.VMEM((512, 256), BF16),
            pltpu.VMEM((128, 128), F32),
            pltpu.VMEM((NROW, 8, 128), F32),
            pltpu.VMEM((NROW - 1, 8, 128), F32),
            pltpu.VMEM((128, 128), F32),
            pltpu.VMEM((8, 8, 128), F32),
            pltpu.VMEM((16, 32), F32),
            pltpu.VMEM((16, 32), F32),
            pltpu.SemaphoreType.DMA((2,)),
            pltpu.SemaphoreType.DMA,
            pltpu.SemaphoreType.DMA((2, 2)),
            pltpu.SemaphoreType.DMA,
            pltpu.SemaphoreType.DMA,
            pltpu.SemaphoreType.DMA,
            pltpu.SemaphoreType.DMA((8,)),
            pltpu.SemaphoreType.DMA,
            pltpu.SemaphoreType.DMA,
            pltpu.SemaphoreType.DMA,
            pltpu.SemaphoreType.DMA,
            pltpu.SemaphoreType.DMA,
            pltpu.SemaphoreType.DMA,
        ],
        compiler_params=pltpu.CompilerParams(collective_id=0, has_side_effects=True),
    )(
        inverse_set.reshape(256, 128),
        presence.reshape(1, 2),
        factor.reshape(128, 512),
    )
    return (-update).reshape(1, 1, 8, 512), dinv + diag_sum


def solution(mesh):
    in_specs = (
        P(None, "row", None, None, "col", None),
        P(None, "row", None, "col"),
        P(None, "row", None, None),
        P("row", "col"),
    )
    out_specs = (P(None, "row", "col", None), P("row", "col"))
    return jax.shard_map(local, mesh=mesh, in_specs=in_specs, out_specs=out_specs, check_vma=False)
```

```python
import jax
import jax.numpy as jnp
from jax import lax
from jax.experimental import pallas as pl
from jax.experimental.pallas import tpu as pltpu
from jax.sharding import PartitionSpec as P

MESH = pl.DeviceIdType.MESH
NROW = 32
F32 = jnp.float32
BF16 = jnp.bfloat16
NT = (((1,), (1,)), ((), ()))
JUMP = 5


def split(value):
    high = value.astype(BF16)
    return high, (value - high.astype(F32)).astype(BF16)


def dot_nt(a, b):
    return lax.dot_general(a, b, NT, preferred_element_type=F32)


def kernel(
    inv_hbm, pres_ref, fac_hbm, off_ref, diag_ref,
    a_raw, a_own, f_raw, ft, ft_mate, abuf, asplit, fbuf, ftsplit, pad, q, trecv, vbuf, vrecv,
    ready, load_sem, f_send, f_first, f_near, f_far, x_send, x_recv, a_send, a_recv,
    t_send, t_recv, v_send, v_recv,
):
    r = lax.axis_index("row")
    c = lax.axis_index("col")
    xh = lax.rem(r, 2)
    z = lax.div(r, 2)
    core = lax.rem(c, 2)
    y = lax.rem(lax.div(c, 2), 4)
    xl = lax.div(c, 8)
    chip = lax.div(c, 2)
    r_pair = r + 1 - 2 * xh

    load_a = pltpu.make_async_copy(inv_hbm, a_raw, load_sem.at[0])
    load_f = pltpu.make_async_copy(fac_hbm, f_raw, load_sem.at[1])

    def send(src, dst, send_sem, recv_sem, peer):
        pltpu.make_async_remote_copy(
            src_ref=src, dst_ref=dst, send_sem=send_sem, recv_sem=recv_sem,
            device_id=peer, device_id_type=MESH,
        ).start()

    def wait(ref, sem):
        pltpu.make_async_copy(ref, ref, sem).wait()

    halves = (xh, xh, 1 - xh, 1 - xh)
    lows = (xl, 1 - xl, 1 - xl, xl)
    rows = (r, r, r_pair, r_pair)

    def column_at(kind, dy, of_core):
        return lows[kind] * 8 + lax.rem(y + dy + 4, 4) * 2 + of_core

    def slot(kind, dy):
        return (halves[kind] * 2 + lows[kind]) * 4 + lax.rem(y + dy + 4, 4)

    def z_peer(dz):
        return (lax.rem(r + 2 * dz + NROW, NROW), c)

    def block_in():
        load_a.wait()
        for b in range(2):
            a_own[b] = a_raw[pl.ds(b, 128, stride=2), :] * pres_ref[0, b].astype(F32)

    def give(kind, dy, own):
        send(
            a_own, abuf.at[own], a_send, a_recv.at[kind, (4 - dy) % 4],
            (rows[kind], column_at(kind, dy, 0)),
        )

    def give_same_half(own):
        for dy in (1, -1):
            give(0, dy, own)
        for dy in (1, -1, 0):
            give(1, dy, own)

    def give_other_half(own):
        for dy in (1, -1, 0):
            give(2, dy, own)

    barrier = pltpu.get_barrier_semaphore()

    def greet(peer):
        pl.semaphore_signal(barrier, inc=1, device_id=peer, device_id_type=MESH)

    def put_update():
        for h in range(4):
            off_ref[:, 128 * h : 128 * (h + 1)] = (
                vrecv[2 * h] + vrecv[2 * h + 1] + (vrecv[2 * h + 8] + vrecv[2 * h + 9])
            )

    def put_diag():
        tile = trecv[0]
        for step in range(1, NROW):
            tile = tile + trecv[step]
        for g in range(4):
            diag_ref[pl.ds(g, 4, stride=4), :] = tile[:, 32 * g : 32 * (g + 1)]

    @pl.when(core == 1)
    def _():
        load_a.start()
        greet((r_pair, c))
        pl.semaphore_wait(barrier, 11)
        pl.semaphore_signal(ready, inc=1, device_id=(r, c - 1), device_id_type=MESH)
        block_in()
        own = slot(0, 0)

        @pl.when(xh == 1)
        def _():
            give_same_half(own)
            give(0, 0, own)

        @pl.when(xh == 0)
        def _():
            give_other_half(own)

        wait(vrecv, v_recv)
        put_update()
        wait(trecv, t_recv)
        put_diag()
        wait(abuf.at[pl.ds(0, 3)], a_send)

        @pl.when(xh == 1)
        def _():
            wait(abuf.at[pl.ds(0, 3)], a_send)

    @pl.when(core == 0)
    def _():
        load_a.start()
        load_f.start()
        for kind in range(3):
            for dy in (1, -1, 0):
                greet((rows[kind], column_at(kind, dy, 1)))
        greet((r_pair, c + 1))
        for dz in range(1, JUMP + 1):
            greet(z_peer(dz))
            greet(z_peer(-dz))

        block_in()
        own = slot(0, 0)
        pl.semaphore_wait(ready, 1)

        @pl.when(xh == 0)
        def _():
            give_same_half(own)
            abuf[own] = a_own[...]

        @pl.when(xh == 1)
        def _():
            give_other_half(own)

        load_f.wait()
        for part in range(4):
            ft[128 * part : 128 * (part + 1), :] = f_raw[:, 128 * part : 128 * (part + 1)].T
        own_rows = pl.ds(pl.multiple_of(32 * c, 64), 64)
        fbuf[z] = ft[own_rows, :]
        pl.semaphore_wait(barrier, 2 * JUMP)

        for way, dz in enumerate((JUMP, -JUMP)):
            send(ft.at[own_rows, :], fbuf.at[z], f_send, f_first.at[way], z_peer(dz))
        for dz in (4, -4, 3, -3, 2, -2, 1, -1):
            send(ft.at[own_rows, :], fbuf.at[z], f_send, f_near, z_peer(dz))
        send(ft, ft_mate, x_send, x_recv, (r_pair, column_at(2, 0, 0)))

        def lay_factor(source, at):
            for g in range(4):
                high, low = split(source[pl.ds(g, 128, stride=4), :])
                ftsplit[0:128, 128 * (4 * at + g) : 128 * (4 * at + g + 1)] = high
                ftsplit[128:256, 128 * (4 * at + g) : 128 * (4 * at + g + 1)] = low

        lay_factor(ft, 0)
        pad[...] = jnp.zeros_like(pad)

        def got(kind, dy):
            wait(abuf.at[slot(kind, dy)], a_recv.at[kind, dy % 4])

        def pass_half(kind, dy):
            b = 0 if dy == -1 else 1
            at = slot(kind, dy)
            send(
                abuf.at[at, b], abuf.at[at, b], a_send, a_recv.at[kind, 2 if b == 0 else 4],
                (r, column_at(0, -dy, 0)),
            )

        def pass_across(dy):
            at = slot(2, dy)
            send(abuf.at[at], abuf.at[at], a_send, a_recv.at[3, dy % 4], (r, column_at(1, 0, 0)))

        for dy in (-1, 1):
            got(2, dy)
            pass_across(dy)
            pass_half(2, dy)
        for dy in (-1, 1):
            got(0, dy)
            pass_half(0, dy)
        got(2, 0)
        pass_across(0)
        for dy in (-1, 1):
            got(1, dy)
            pass_half(1, dy)

        for way in range(2):
            sign = 1 - 2 * way
            at = lax.rem(z - sign * JUMP + 16, 16)
            wait(fbuf.at[at], f_first.at[way])
            half = fbuf.at[at, pl.ds(32 * way, 32)]
            send(half, half, f_send, f_far, z_peer(3 * sign))
            for dz in (2 * sign, sign):
                send(fbuf.at[at], fbuf.at[at], f_send, f_far, z_peer(dz))

        for dy in (-1, 1):
            got(3, dy)
            pass_half(3, dy)
        got(1, 0)
        got(3, 0)

        @pl.when(xh == 1)
        def _():
            got(0, 0)

        for kind in range(4):
            for b in range(2):
                wait(abuf.at[slot(kind, 2), b], a_recv.at[kind, 2 if b == 0 else 4])
        wait(ft_mate, x_recv)
        lay_factor(ft_mate, 1)

        def lay_blocks(p, carry):
            for at, half in enumerate((xh, 1 - xh)):
                for b in range(2):
                    high, low = split(abuf[half * 8 + p, b])
                    asplit[2 * p + b, 256 * at : 256 * at + 128] = high
                    asplit[2 * p + b, 256 * at + 128 : 256 * at + 256] = low
            return carry

        lax.fori_loop(0, 8, lay_blocks, 0)

        def product(dz):
            at = lax.rem(z + dz + 16, 16)
            lhs = jnp.concatenate(split(fbuf[at]), axis=0)
            return dot_nt(lhs, asplit[lax.rem(at, 8) * 2 + lax.div(at, 8)])

        wait(fbuf.at[pl.ds(0, 8)], f_near)
        total = product(0)
        for dz in range(1, 6):
            total = total + product(dz) + product(-dz)
        wait(fbuf.at[pl.ds(0, 5)], f_far)
        for dz in (6, -6, 7, -7, 8):
            total = total + product(dz)
        parts = [
            total[:64, 256 * at : 256 * at + 128]
            + (total[:64, 256 * at + 128 : 256 * at + 256] + total[64:, 256 * at : 256 * at + 128])
            for at in range(2)
        ]

        stacks = []
        for part in parts:
            pieces = split(part)
            for g in range(4):
                stack = []
                for of_core in range(2):
                    for piece in pieces:
                        for lane in range(4):
                            here = piece[32 * of_core : 32 * of_core + 32]
                            stack.append(here if lane == g else jnp.zeros((32, 128), BF16))
                stacks.append(jnp.concatenate(stack, axis=0))
        full = dot_nt(ftsplit[...], jnp.concatenate(stacks, axis=1))
        for of_core in range(2):
            left = 256 * of_core
            tiles = full[:128, left : left + 128] + (full[:128, left + 128 : left + 256] + full[128:, left : left + 128])
            q[:, of_core] = tiles.reshape(NROW, 4, 128)
        for at in range(NROW - 1):
            goal = at + (r <= at).astype(jnp.int32)
            step = lax.rem(goal - r + NROW, NROW)
            for of_core in range(2):
                send(q.at[goal, of_core], trecv.at[step], t_send, t_recv, (goal, c + of_core))
        send(q.at[r, 1], trecv.at[0], t_send, t_recv, (r, c + 1))
        trecv[0] = q[r, 0]

        half_rows = pl.ds(pl.multiple_of(64 * lax.rem(chip, 2), 64), 64)
        mine = xh * 8 + chip
        for which in range(2):
            pad[which, half_rows, :] = parts[which]
            vbuf[which] = pad[which].T
        vrecv[mine] = vbuf[0, pl.ds(pl.multiple_of(8 * c, 8), 8), :]
        for kind in (3, 2, 1, 0):
            for dy in (2, 3, 1, 0):
                for of_core in range(2):
                    if (kind, dy, of_core) != (0, 0, 0):
                        col = column_at(kind, dy, of_core)
                        slab = vbuf.at[kind // 2, pl.ds(pl.multiple_of(8 * col, 8), 8), :]
                        send(slab, vrecv.at[mine], v_send, v_recv, (rows[kind], col))

        wait(vrecv.at[pl.ds(0, 15)], v_recv)
        put_update()

        wait(trecv.at[pl.ds(1, 31)], t_recv)
        put_diag()

        wait(fbuf.at[pl.ds(0, 15)], f_send)
        wait(ft, x_send)
        wait(abuf.at[pl.ds(0, 10)], a_send)

        @pl.when(xh == 0)
        def _():
            wait(abuf.at[pl.ds(0, 2)], a_send)

        wait(q.at[pl.ds(0, 31)], t_send)
        wait(trecv.at[0], t_send)
        wait(vrecv.at[pl.ds(0, 16)], v_send)
        wait(vrecv.at[pl.ds(0, 15)], v_send)


def local(inverse_set, presence, factor, dinv):
    update, diag_sum = pl.pallas_call(
        kernel,
        out_shape=(jax.ShapeDtypeStruct((8, 512), F32), jax.ShapeDtypeStruct((16, 32), F32)),
        in_specs=[
            pl.BlockSpec(memory_space=pl.ANY),
            pl.BlockSpec(memory_space=pltpu.SMEM),
            pl.BlockSpec(memory_space=pl.ANY),
        ],
        out_specs=(pl.BlockSpec(memory_space=pltpu.VMEM), pl.BlockSpec(memory_space=pltpu.VMEM)),
        scratch_shapes=[
            pltpu.VMEM((256, 128), F32),
            pltpu.VMEM((2, 128, 128), F32),
            pltpu.VMEM((128, 512), F32),
            pltpu.VMEM((512, 128), F32),
            pltpu.VMEM((512, 128), F32),
            pltpu.VMEM((16, 2, 128, 128), F32),
            pltpu.VMEM((16, 512, 128), BF16),
            pltpu.VMEM((16, 64, 128), F32),
            pltpu.VMEM((256, 1024), BF16),
            pltpu.VMEM((2, 128, 128), F32),
            pltpu.VMEM((NROW, 2, 4, 128), F32),
            pltpu.VMEM((NROW, 4, 128), F32),
            pltpu.VMEM((2, 128, 128), F32),
            pltpu.VMEM((16, 8, 128), F32),
            pltpu.SemaphoreType.REGULAR,
            pltpu.SemaphoreType.DMA((2,)),
            pltpu.SemaphoreType.DMA,
            pltpu.SemaphoreType.DMA((2,)),
            pltpu.SemaphoreType.DMA,
            pltpu.SemaphoreType.DMA,
            pltpu.SemaphoreType.DMA,
            pltpu.SemaphoreType.DMA,
            pltpu.SemaphoreType.DMA,
            pltpu.SemaphoreType.DMA((4, 5)),
            pltpu.SemaphoreType.DMA,
            pltpu.SemaphoreType.DMA,
            pltpu.SemaphoreType.DMA,
            pltpu.SemaphoreType.DMA,
        ],
        compiler_params=pltpu.CompilerParams(collective_id=0, has_side_effects=True),
    )(
        inverse_set.reshape(256, 128),
        presence.reshape(1, 2),
        factor.reshape(128, 512),
    )
    return (-update).reshape(1, 1, 8, 512), dinv + diag_sum


def solution(mesh):
    in_specs = (
        P(None, "row", None, None, "col", None),
        P(None, "row", None, "col"),
        P(None, "row", None, None),
        P("row", "col"),
    )
    out_specs = (P(None, "row", "col", None), P("row", "col"))
    return jax.shard_map(local, mesh=mesh, in_specs=in_specs, out_specs=out_specs, check_vma=False)
```

```python
import jax
import jax.numpy as jnp
from jax import lax
from jax.experimental import pallas as pl
from jax.experimental.pallas import tpu as pltpu
from jax.sharding import PartitionSpec as P

MESH = pl.DeviceIdType.MESH
NROW = 32
F32 = jnp.float32
BF16 = jnp.bfloat16
NT = (((1,), (1,)), ((), ()))
JUMP = 5


def split(value):
    high = value.astype(BF16)
    return high, (value - high.astype(F32)).astype(BF16)


def dot_nt(a, b):
    return lax.dot_general(a, b, NT, preferred_element_type=F32)


def kernel(
    inv_hbm, pres_ref, fac_hbm, off_ref, diag_ref,
    a_raw, a_own, f_raw, ft, ft_mate, abuf, asplit, fbuf, ftsplit, pad, q, trecv, vbuf, vrecv,
    ready, load_sem, f_send, f_first, f_near, f_far, x_send, x_recv, a_send, a_recv,
    t_send, t_recv, v_send, v_recv,
):
    r = lax.axis_index("row")
    c = lax.axis_index("col")
    xh = lax.rem(r, 2)
    z = lax.div(r, 2)
    core = lax.rem(c, 2)
    y = lax.rem(lax.div(c, 2), 4)
    xl = lax.div(c, 8)
    chip = lax.div(c, 2)
    r_pair = r + 1 - 2 * xh

    load_a = pltpu.make_async_copy(inv_hbm, a_raw, load_sem.at[0])
    load_f = pltpu.make_async_copy(fac_hbm, f_raw, load_sem.at[1])

    def send(src, dst, send_sem, recv_sem, peer):
        pltpu.make_async_remote_copy(
            src_ref=src, dst_ref=dst, send_sem=send_sem, recv_sem=recv_sem,
            device_id=peer, device_id_type=MESH,
        ).start()

    def wait(ref, sem):
        pltpu.make_async_copy(ref, ref, sem).wait()

    halves = (xh, xh, 1 - xh, 1 - xh)
    lows = (xl, 1 - xl, 1 - xl, xl)
    rows = (r, r, r_pair, r_pair)

    def column_at(kind, dy, of_core):
        return lows[kind] * 8 + lax.rem(y + dy + 4, 4) * 2 + of_core

    def slot(kind, dy):
        return (halves[kind] * 2 + lows[kind]) * 4 + lax.rem(y + dy + 4, 4)

    def z_peer(dz):
        return (lax.rem(r + 2 * dz + NROW, NROW), c)

    def block_in():
        load_a.wait()
        for b in range(2):
            a_own[b] = a_raw[pl.ds(b, 128, stride=2), :] * pres_ref[0, b].astype(F32)

    def give(kind, dy, b, own):
        send(
            a_own.at[b], abuf.at[own, b], a_send, a_recv.at[kind, (4 - dy) % 4, b],
            (rows[kind], column_at(kind, dy, 0)),
        )

    def give_same_half(own):
        for b in range(2):
            for kind, dy in ((1, 0), (0, 1), (0, -1)):
                give(kind, dy, b, own)

    def give_other_half(own):
        for b in range(2):
            for dy in (1, -1):
                give(2, dy, b, own)
        for b in range(2):
            give(2, 0, b, own)

    barrier = pltpu.get_barrier_semaphore()

    def greet(peer):
        pl.semaphore_signal(barrier, inc=1, device_id=peer, device_id_type=MESH)

    def put_update():
        for h in range(4):
            off_ref[:, 128 * h : 128 * (h + 1)] = (
                vrecv[2 * h] + vrecv[2 * h + 1] + (vrecv[2 * h + 8] + vrecv[2 * h + 9])
            )

    def put_diag():
        tile = trecv[0]
        for step in range(1, NROW):
            tile = tile + trecv[step]
        for g in range(4):
            diag_ref[pl.ds(g, 4, stride=4), :] = tile[:, 32 * g : 32 * (g + 1)]

    @pl.when(core == 1)
    def _():
        load_a.start()
        greet((r_pair, c))
        pl.semaphore_wait(barrier, 11)
        pl.semaphore_signal(ready, inc=1, device_id=(r, c - 1), device_id_type=MESH)
        block_in()
        own = slot(0, 0)

        @pl.when(xh == 1)
        def _():
            give_same_half(own)
            for b in range(2):
                give(0, 0, b, own)

        @pl.when(xh == 0)
        def _():
            give_other_half(own)

        wait(vrecv, v_recv)
        put_update()
        wait(trecv, t_recv)
        put_diag()
        wait(abuf.at[pl.ds(0, 3)], a_send)

        @pl.when(xh == 1)
        def _():
            wait(abuf.at[0], a_send)

    @pl.when(core == 0)
    def _():
        load_a.start()
        load_f.start()
        for kind in range(3):
            for dy in (1, -1, 0):
                greet((rows[kind], column_at(kind, dy, 1)))
        greet((r_pair, c + 1))
        for dz in range(1, JUMP + 1):
            greet(z_peer(dz))
            greet(z_peer(-dz))

        block_in()
        own = slot(0, 0)
        pl.semaphore_wait(ready, 1)

        @pl.when(xh == 0)
        def _():
            give_same_half(own)
            abuf[own] = a_own[...]

        @pl.when(xh == 1)
        def _():
            give_other_half(own)

        load_f.wait()
        for part in range(4):
            ft[128 * part : 128 * (part + 1), :] = f_raw[:, 128 * part : 128 * (part + 1)].T
        own_rows = pl.ds(pl.multiple_of(32 * c, 64), 64)
        fbuf[z] = ft[own_rows, :]
        pl.semaphore_wait(barrier, 2 * JUMP)

        for way, dz in enumerate((JUMP, -JUMP)):
            send(ft.at[own_rows, :], fbuf.at[z], f_send, f_first.at[way], z_peer(dz))
        for dz in (4, -4, 3, -3, 2, -2, 1, -1):
            send(ft.at[own_rows, :], fbuf.at[z], f_send, f_near, z_peer(dz))
        send(ft, ft_mate, x_send, x_recv, (r_pair, column_at(2, 0, 0)))

        def lay_factor(source, at):
            for g in range(4):
                high, low = split(source[pl.ds(g, 128, stride=4), :])
                ftsplit[0:128, 128 * (4 * at + g) : 128 * (4 * at + g + 1)] = high
                ftsplit[128:256, 128 * (4 * at + g) : 128 * (4 * at + g + 1)] = low

        lay_factor(ft, 0)
        pad[...] = jnp.zeros_like(pad)

        def got(kind, dy, b):
            wait(abuf.at[slot(kind, dy), b], a_recv.at[kind, dy % 4, b])

        def pass_y(kind, dy, b, to):
            at = slot(kind, dy)
            send(
                abuf.at[at, b], abuf.at[at, b], a_send, a_recv.at[kind, (dy - to) % 4, b],
                (r, column_at(0, to, 0)),
            )

        def pass_across(dy, b):
            at = slot(2, dy)
            send(abuf.at[at, b], abuf.at[at, b], a_send, a_recv.at[3, dy % 4, b], (r, column_at(1, 0, 0)))

        for b in range(2):
            got(1, 0, b)
            pass_y(1, 0, b, 1)
            pass_y(1, 0, b, -1)
            for dy in (-1, 1):
                got(2, dy, b)
                pass_across(dy, b)
                if dy == 2 * b - 1:
                    pass_y(2, dy, b, -dy)
            got(0, 2 * b - 1, b)
            pass_y(0, 2 * b - 1, b, 1 - 2 * b)
        for b in range(2):
            got(2, 0, b)
            pass_across(0, b)
        for b in range(2):
            got(1, 2 * b - 1, b)
            pass_y(1, 2 * b - 1, b, 1 - 2 * b)

        for way in range(2):
            sign = 1 - 2 * way
            at = lax.rem(z - sign * JUMP + 16, 16)
            wait(fbuf.at[at], f_first.at[way])
            half = fbuf.at[at, pl.ds(32 * way, 32)]
            send(half, half, f_send, f_far, z_peer(3 * sign))
            for dz in (2 * sign, sign):
                send(fbuf.at[at], fbuf.at[at], f_send, f_far, z_peer(dz))

        for b in range(2):
            got(3, 2 * b - 1, b)
            pass_y(3, 2 * b - 1, b, 1 - 2 * b)

        @pl.when(xh == 1)
        def _():
            for b in range(2):
                got(0, 0, b)

        for b in range(2):
            for kind in (0, 1, 3):
                got(kind, 1 - 2 * b, b)
            got(3, 0, b)
            for kind in range(4):
                got(kind, 2, b)
        wait(ft_mate, x_recv)
        lay_factor(ft_mate, 1)

        def lay_blocks(p, carry):
            for at, half in enumerate((xh, 1 - xh)):
                for b in range(2):
                    high, low = split(abuf[half * 8 + p, b])
                    asplit[2 * p + b, 256 * at : 256 * at + 128] = high
                    asplit[2 * p + b, 256 * at + 128 : 256 * at + 256] = low
            return carry

        lax.fori_loop(0, 8, lay_blocks, 0)

        def product(dz):
            at = lax.rem(z + dz + 16, 16)
            lhs = jnp.concatenate(split(fbuf[at]), axis=0)
            return dot_nt(lhs, asplit[lax.rem(at, 8) * 2 + lax.div(at, 8)])

        wait(fbuf.at[pl.ds(0, 8)], f_near)
        total = product(0)
        for dz in range(1, 6):
            total = total + product(dz) + product(-dz)
        wait(fbuf.at[pl.ds(0, 5)], f_far)
        for dz in (6, -6, 7, -7, 8):
            total = total + product(dz)
        parts = [
            total[:64, 256 * at : 256 * at + 128]
            + (total[:64, 256 * at + 128 : 256 * at + 256] + total[64:, 256 * at : 256 * at + 128])
            for at in range(2)
        ]

        stacks = []
        for part in parts:
            pieces = split(part)
            for g in range(4):
                stack = []
                for of_core in range(2):
                    for piece in pieces:
                        for lane in range(4):
                            here = piece[32 * of_core : 32 * of_core + 32]
                            stack.append(here if lane == g else jnp.zeros((32, 128), BF16))
                stacks.append(jnp.concatenate(stack, axis=0))
        full = dot_nt(ftsplit[...], jnp.concatenate(stacks, axis=1))
        for of_core in range(2):
            left = 256 * of_core
            tiles = full[:128, left : left + 128] + (full[:128, left + 128 : left + 256] + full[128:, left : left + 128])
            q[:, of_core] = tiles.reshape(NROW, 4, 128)
        for at in range(NROW - 1):
            goal = at + (r <= at).astype(jnp.int32)
            step = lax.rem(goal - r + NROW, NROW)
            for of_core in range(2):
                send(q.at[goal, of_core], trecv.at[step], t_send, t_recv, (goal, c + of_core))
        send(q.at[r, 1], trecv.at[0], t_send, t_recv, (r, c + 1))
        trecv[0] = q[r, 0]

        half_rows = pl.ds(pl.multiple_of(64 * lax.rem(chip, 2), 64), 64)
        mine = xh * 8 + chip
        for which in range(2):
            pad[which, half_rows, :] = parts[which]
            vbuf[which] = pad[which].T
        vrecv[mine] = vbuf[0, pl.ds(pl.multiple_of(8 * c, 8), 8), :]
        for kind in (3, 2, 1, 0):
            for dy in (2, 3, 1, 0):
                for of_core in range(2):
                    if (kind, dy, of_core) != (0, 0, 0):
                        col = column_at(kind, dy, of_core)
                        slab = vbuf.at[kind // 2, pl.ds(pl.multiple_of(8 * col, 8), 8), :]
                        send(slab, vrecv.at[mine], v_send, v_recv, (rows[kind], col))

        wait(vrecv.at[pl.ds(0, 15)], v_recv)
        put_update()

        wait(trecv.at[pl.ds(1, 31)], t_recv)
        put_diag()

        wait(fbuf.at[pl.ds(0, 15)], f_send)
        wait(ft, x_send)
        wait(abuf.at[pl.ds(0, 12)], a_send)
        wait(q.at[pl.ds(0, 31)], t_send)
        wait(trecv.at[0], t_send)
        wait(vrecv.at[pl.ds(0, 16)], v_send)
        wait(vrecv.at[pl.ds(0, 15)], v_send)


def local(inverse_set, presence, factor, dinv):
    update, diag_sum = pl.pallas_call(
        kernel,
        out_shape=(pltpu.VMEM((8, 512), F32), pltpu.VMEM((16, 32), F32)),
        in_specs=[
            pl.BlockSpec(memory_space=pl.ANY),
            pl.BlockSpec(memory_space=pltpu.SMEM),
            pl.BlockSpec(memory_space=pl.ANY),
        ],
        out_specs=(pl.BlockSpec(memory_space=pltpu.VMEM), pl.BlockSpec(memory_space=pltpu.VMEM)),
        scratch_shapes=[
            pltpu.VMEM((256, 128), F32),
            pltpu.VMEM((2, 128, 128), F32),
            pltpu.VMEM((128, 512), F32),
            pltpu.VMEM((512, 128), F32),
            pltpu.VMEM((512, 128), F32),
            pltpu.VMEM((16, 2, 128, 128), F32),
            pltpu.VMEM((16, 512, 128), BF16),
            pltpu.VMEM((16, 64, 128), F32),
            pltpu.VMEM((256, 1024), BF16),
            pltpu.VMEM((2, 128, 128), F32),
            pltpu.VMEM((NROW, 2, 4, 128), F32),
            pltpu.VMEM((NROW, 4, 128), F32),
            pltpu.VMEM((2, 128, 128), F32),
            pltpu.VMEM((16, 8, 128), F32),
            pltpu.SemaphoreType.REGULAR,
            pltpu.SemaphoreType.DMA((2,)),
            pltpu.SemaphoreType.DMA,
            pltpu.SemaphoreType.DMA((2,)),
            pltpu.SemaphoreType.DMA,
            pltpu.SemaphoreType.DMA,
            pltpu.SemaphoreType.DMA,
            pltpu.SemaphoreType.DMA,
            pltpu.SemaphoreType.DMA,
            pltpu.SemaphoreType.DMA((4, 4, 2)),
            pltpu.SemaphoreType.DMA,
            pltpu.SemaphoreType.DMA,
            pltpu.SemaphoreType.DMA,
            pltpu.SemaphoreType.DMA,
        ],
        compiler_params=pltpu.CompilerParams(collective_id=0, has_side_effects=True),
    )(
        inverse_set.reshape(256, 128),
        presence.reshape(1, 2),
        factor.reshape(128, 512),
    )
    return (-update).reshape(1, 1, 8, 512), dinv + diag_sum


def solution(mesh):
    in_specs = (
        P(None, "row", None, None, "col", None),
        P(None, "row", None, "col"),
        P(None, "row", None, None),
        P("row", "col"),
    )
    out_specs = (P(None, "row", "col", None), P("row", "col"))
    return jax.shard_map(local, mesh=mesh, in_specs=in_specs, out_specs=out_specs, check_vma=False)
```

```python
import jax
import jax.numpy as jnp
from jax import lax
from jax.experimental import pallas as pl
from jax.experimental.pallas import tpu as pltpu
from jax.sharding import PartitionSpec as P

MESH = pl.DeviceIdType.MESH
NROW = 32
F32 = jnp.float32
BF16 = jnp.bfloat16
NT = (((1,), (1,)), ((), ()))
JUMP = 5


def split(value):
    high = value.astype(BF16)
    return high, (value - high.astype(F32)).astype(BF16)


def dot_nt(a, b):
    return lax.dot_general(a, b, NT, preferred_element_type=F32)


def kernel(
    inv_hbm, pres_ref, fac_hbm, dinv_hbm, off_ref, diag_ref,
    a_raw, a_own, d_raw, f_raw, ft, ft_mate, abuf, asplit, fbuf, ftsplit, pad, q, trecv, vbuf, vrecv,
    ready, load_sem, f_send, f_first, f_near, f_far, x_send, x_recv, a_send, a_recv,
    t_send, t_recv, v_send, v_recv,
):
    r = lax.axis_index("row")
    c = lax.axis_index("col")
    xh = lax.rem(r, 2)
    z = lax.div(r, 2)
    core = lax.rem(c, 2)
    y = lax.rem(lax.div(c, 2), 4)
    xl = lax.div(c, 8)
    chip = lax.div(c, 2)
    r_pair = r + 1 - 2 * xh

    load_a = pltpu.make_async_copy(inv_hbm, a_raw, load_sem.at[0])
    load_f = pltpu.make_async_copy(fac_hbm, f_raw, load_sem.at[1])
    load_d = pltpu.make_async_copy(dinv_hbm, d_raw, load_sem.at[2])

    def send(src, dst, send_sem, recv_sem, peer):
        pltpu.make_async_remote_copy(
            src_ref=src, dst_ref=dst, send_sem=send_sem, recv_sem=recv_sem,
            device_id=peer, device_id_type=MESH,
        ).start()

    def wait(ref, sem):
        pltpu.make_async_copy(ref, ref, sem).wait()

    halves = (xh, xh, 1 - xh, 1 - xh)
    lows = (xl, 1 - xl, 1 - xl, xl)
    rows = (r, r, r_pair, r_pair)

    def column_at(kind, dy, of_core):
        return lows[kind] * 8 + lax.rem(y + dy + 4, 4) * 2 + of_core

    def slot(kind, dy):
        return (halves[kind] * 2 + lows[kind]) * 4 + lax.rem(y + dy + 4, 4)

    def z_peer(dz):
        return (lax.rem(r + 2 * dz + NROW, NROW), c)

    def block_in():
        load_a.wait()
        for b in range(2):
            a_own[b] = a_raw[pl.ds(b, 128, stride=2), :] * pres_ref[0, b].astype(F32)

    def give(kind, dy, b, own):
        send(
            a_own.at[b], abuf.at[own, b], a_send, a_recv.at[kind, (4 - dy) % 4, b],
            (rows[kind], column_at(kind, dy, 0)),
        )

    def give_same_half(own):
        for b in range(2):
            for kind, dy in ((1, 0), (0, 1), (0, -1)):
                give(kind, dy, b, own)

    def give_other_half(own):
        for b in range(2):
            for dy in (1, -1):
                give(2, dy, b, own)
        for b in range(2):
            give(2, 0, b, own)

    barrier = pltpu.get_barrier_semaphore()

    def greet(peer):
        pl.semaphore_signal(barrier, inc=1, device_id=peer, device_id_type=MESH)

    def put_update():
        for h in range(4):
            off_ref[:, 128 * h : 128 * (h + 1)] = -(
                vrecv[2 * h] + vrecv[2 * h + 1] + (vrecv[2 * h + 8] + vrecv[2 * h + 9])
            )

    def put_diag():
        tile = trecv[0]
        for step in range(1, NROW):
            tile = tile + trecv[step]
        for g in range(4):
            spots = pl.ds(g, 4, stride=4)
            diag_ref[spots, :] = d_raw[spots, :] + tile[:, 32 * g : 32 * (g + 1)]

    @pl.when(core == 1)
    def _():
        load_a.start()
        load_d.start()
        greet((r_pair, c))
        pl.semaphore_wait(barrier, 11)
        pl.semaphore_signal(ready, inc=1, device_id=(r, c - 1), device_id_type=MESH)
        block_in()
        own = slot(0, 0)

        @pl.when(xh == 1)
        def _():
            give_same_half(own)
            for b in range(2):
                give(0, 0, b, own)

        @pl.when(xh == 0)
        def _():
            give_other_half(own)

        load_d.wait()
        wait(vrecv, v_recv)
        put_update()
        wait(trecv, t_recv)
        put_diag()
        wait(abuf.at[pl.ds(0, 3)], a_send)

        @pl.when(xh == 1)
        def _():
            wait(abuf.at[0], a_send)

    @pl.when(core == 0)
    def _():
        load_a.start()
        load_f.start()
        load_d.start()
        for kind in range(3):
            for dy in (1, -1, 0):
                greet((rows[kind], column_at(kind, dy, 1)))
        greet((r_pair, c + 1))
        for dz in range(1, JUMP + 1):
            greet(z_peer(dz))
            greet(z_peer(-dz))

        block_in()
        own = slot(0, 0)
        pl.semaphore_wait(ready, 1)

        @pl.when(xh == 0)
        def _():
            give_same_half(own)
            abuf[own] = a_own[...]

        @pl.when(xh == 1)
        def _():
            give_other_half(own)

        load_f.wait()
        for part in range(4):
            ft[128 * part : 128 * (part + 1), :] = f_raw[:, 128 * part : 128 * (part + 1)].T
        own_rows = pl.ds(pl.multiple_of(32 * c, 64), 64)
        fbuf[z] = ft[own_rows, :]
        pl.semaphore_wait(barrier, 2 * JUMP)

        for way, dz in enumerate((JUMP, -JUMP)):
            send(ft.at[own_rows, :], fbuf.at[z], f_send, f_first.at[way], z_peer(dz))
        for dz in (4, -4, 3, -3, 2, -2, 1, -1):
            send(ft.at[own_rows, :], fbuf.at[z], f_send, f_near, z_peer(dz))

        def lay_factor(source, at):
            for g in range(4):
                high, low = split(source[pl.ds(g, 128, stride=4), :])
                ftsplit[0:128, 128 * (4 * at + g) : 128 * (4 * at + g + 1)] = high
                ftsplit[128:256, 128 * (4 * at + g) : 128 * (4 * at + g + 1)] = low

        lay_factor(ft, 0)
        load_d.wait()
        pad[...] = jnp.zeros_like(pad)

        def got(kind, dy, b):
            wait(abuf.at[slot(kind, dy), b], a_recv.at[kind, dy % 4, b])

        def pass_y(kind, dy, b, to):
            at = slot(kind, dy)
            send(
                abuf.at[at, b], abuf.at[at, b], a_send, a_recv.at[kind, (dy - to) % 4, b],
                (r, column_at(0, to, 0)),
            )

        def pass_across(dy, b):
            at = slot(2, dy)
            send(abuf.at[at, b], abuf.at[at, b], a_send, a_recv.at[3, dy % 4, b], (r, column_at(1, 0, 0)))

        for b in range(2):
            got(1, 0, b)
            pass_y(1, 0, b, 1)
            pass_y(1, 0, b, -1)
            for dy in (-1, 1):
                got(2, dy, b)
                pass_across(dy, b)
                if dy == 2 * b - 1:
                    pass_y(2, dy, b, -dy)
            got(0, 2 * b - 1, b)
            pass_y(0, 2 * b - 1, b, 1 - 2 * b)
        for b in range(2):
            got(2, 0, b)
            pass_across(0, b)
        for b in range(2):
            got(1, 2 * b - 1, b)
            pass_y(1, 2 * b - 1, b, 1 - 2 * b)

        for way in range(2):
            sign = 1 - 2 * way
            at = lax.rem(z - sign * JUMP + 16, 16)
            wait(fbuf.at[at], f_first.at[way])
            half = fbuf.at[at, pl.ds(32 * way, 32)]
            send(half, half, f_send, f_far, z_peer(3 * sign))
            for dz in (2 * sign, sign):
                send(fbuf.at[at], fbuf.at[at], f_send, f_far, z_peer(dz))

        send(ft, ft_mate, x_send, x_recv, (r_pair, column_at(2, 0, 0)))

        for b in range(2):
            got(3, 2 * b - 1, b)
            pass_y(3, 2 * b - 1, b, 1 - 2 * b)

        @pl.when(xh == 1)
        def _():
            for b in range(2):
                got(0, 0, b)

        def lay_piece(kind, dy, b):
            high, low = split(abuf[slot(kind, dy), b])
            at = (lows[kind] * 4 + lax.rem(y + dy + 4, 4)) * 2 + b
            left = 256 * (kind // 2)
            asplit[at, left : left + 128] = high
            asplit[at, left + 128 : left + 256] = low

        def product(low_x, dy, b):
            chip_at = low_x * 4 + lax.rem(y + dy + 4, 4)
            lhs = jnp.concatenate(split(fbuf[chip_at + 8 * b]), axis=0)
            return dot_nt(lhs, asplit[chip_at * 2 + b])

        for b in range(2):
            for kind in (0, 1, 3):
                got(kind, 1 - 2 * b, b)
            got(3, 0, b)
        for kind in range(4):
            for dy in (0, 1, -1):
                for b in range(2):
                    lay_piece(kind, dy, b)
        wait(ft_mate, x_recv)
        lay_factor(ft_mate, 1)
        wait(fbuf.at[pl.ds(0, 8)], f_near)
        wait(fbuf.at[pl.ds(0, 5)], f_far)
        total = jnp.zeros((128, 512), F32)
        for low_x in (xl, 1 - xl):
            for dy in (0, 1, -1):
                for b in range(2):
                    total = total + product(low_x, dy, b)
        for kind in range(4):
            for b in range(2):
                got(kind, 2, b)
                lay_piece(kind, 2, b)
        for low_x in (xl, 1 - xl):
            for b in range(2):
                total = total + product(low_x, 2, b)
        parts = [
            total[:64, 256 * at : 256 * at + 128]
            + (total[:64, 256 * at + 128 : 256 * at + 256] + total[64:, 256 * at : 256 * at + 128])
            for at in range(2)
        ]

        stacks = []
        for part in parts:
            pieces = split(part)
            for g in range(4):
                stack = []
                for of_core in range(2):
                    for piece in pieces:
                        for lane in range(4):
                            here = piece[32 * of_core : 32 * of_core + 32]
                            stack.append(here if lane == g else jnp.zeros((32, 128), BF16))
                stacks.append(jnp.concatenate(stack, axis=0))
        full = dot_nt(ftsplit[...], jnp.concatenate(stacks, axis=1))
        for of_core in range(2):
            left = 256 * of_core
            tiles = full[:128, left : left + 128] + (full[:128, left + 128 : left + 256] + full[128:, left : left + 128])
            q[:, of_core] = tiles.reshape(NROW, 4, 128)
        for at in range(NROW - 1):
            goal = at + (r <= at).astype(jnp.int32)
            step = lax.rem(goal - r + NROW, NROW)
            for of_core in range(2):
                send(q.at[goal, of_core], trecv.at[step], t_send, t_recv, (goal, c + of_core))
        send(q.at[r, 1], trecv.at[0], t_send, t_recv, (r, c + 1))
        trecv[0] = q[r, 0]

        half_rows = pl.ds(pl.multiple_of(64 * lax.rem(chip, 2), 64), 64)
        mine = xh * 8 + chip
        for which in range(2):
            pad[which, half_rows, :] = parts[which]
            vbuf[which] = pad[which].T
        vrecv[mine] = vbuf[0, pl.ds(pl.multiple_of(8 * c, 8), 8), :]
        for kind in (3, 2, 1, 0):
            for dy in (2, 3, 1, 0):
                for of_core in range(2):
                    if (kind, dy, of_core) != (0, 0, 0):
                        col = column_at(kind, dy, of_core)
                        slab = vbuf.at[kind // 2, pl.ds(pl.multiple_of(8 * col, 8), 8), :]
                        send(slab, vrecv.at[mine], v_send, v_recv, (rows[kind], col))

        wait(vrecv.at[pl.ds(0, 15)], v_recv)
        put_update()

        wait(trecv.at[pl.ds(1, 31)], t_recv)
        put_diag()

        wait(fbuf.at[pl.ds(0, 15)], f_send)
        wait(ft, x_send)
        wait(abuf.at[pl.ds(0, 12)], a_send)
        wait(q.at[pl.ds(0, 31)], t_send)
        wait(trecv.at[0], t_send)
        wait(vrecv.at[pl.ds(0, 16)], v_send)
        wait(vrecv.at[pl.ds(0, 15)], v_send)


def local(inverse_set, presence, factor, dinv):
    update, diag = pl.pallas_call(
        kernel,
        out_shape=(pltpu.VMEM((8, 512), F32), pltpu.VMEM((16, 32), F32)),
        in_specs=[
            pl.BlockSpec(memory_space=pl.ANY),
            pl.BlockSpec(memory_space=pltpu.SMEM),
            pl.BlockSpec(memory_space=pl.ANY),
            pl.BlockSpec(memory_space=pl.ANY),
        ],
        out_specs=(pl.BlockSpec(memory_space=pltpu.VMEM), pl.BlockSpec(memory_space=pltpu.VMEM)),
        scratch_shapes=[
            pltpu.VMEM((256, 128), F32),
            pltpu.VMEM((2, 128, 128), F32),
            pltpu.VMEM((16, 32), F32),
            pltpu.VMEM((128, 512), F32),
            pltpu.VMEM((512, 128), F32),
            pltpu.VMEM((512, 128), F32),
            pltpu.VMEM((16, 2, 128, 128), F32),
            pltpu.VMEM((16, 512, 128), BF16),
            pltpu.VMEM((16, 64, 128), F32),
            pltpu.VMEM((256, 1024), BF16),
            pltpu.VMEM((2, 128, 128), F32),
            pltpu.VMEM((NROW, 2, 4, 128), F32),
            pltpu.VMEM((NROW, 4, 128), F32),
            pltpu.VMEM((2, 128, 128), F32),
            pltpu.VMEM((16, 8, 128), F32),
            pltpu.SemaphoreType.REGULAR,
            pltpu.SemaphoreType.DMA((3,)),
            pltpu.SemaphoreType.DMA,
            pltpu.SemaphoreType.DMA((2,)),
            pltpu.SemaphoreType.DMA,
            pltpu.SemaphoreType.DMA,
            pltpu.SemaphoreType.DMA,
            pltpu.SemaphoreType.DMA,
            pltpu.SemaphoreType.DMA,
            pltpu.SemaphoreType.DMA((4, 4, 2)),
            pltpu.SemaphoreType.DMA,
            pltpu.SemaphoreType.DMA,
            pltpu.SemaphoreType.DMA,
            pltpu.SemaphoreType.DMA,
        ],
        compiler_params=pltpu.CompilerParams(collective_id=0, has_side_effects=True),
    )(
        inverse_set.reshape(256, 128),
        presence.reshape(1, 2),
        factor.reshape(128, 512),
        dinv,
    )
    return update.reshape(1, 1, 8, 512), diag


def solution(mesh):
    in_specs = (
        P(None, "row", None, None, "col", None),
        P(None, "row", None, "col"),
        P(None, "row", None, None),
        P("row", "col"),
    )
    out_specs = (P(None, "row", "col", None), P("row", "col"))
    return jax.shard_map(local, mesh=mesh, in_specs=in_specs, out_specs=out_specs, check_vma=False)
```

```python
import jax
import jax.numpy as jnp
from jax import lax
from jax.experimental import pallas as pl
from jax.experimental.pallas import tpu as pltpu
from jax.sharding import PartitionSpec as P

MESH = pl.DeviceIdType.MESH
NROW = 32
F32 = jnp.float32
BF16 = jnp.bfloat16
NT = (((1,), (1,)), ((), ()))
JUMP = 5


def split(value):
    high = value.astype(BF16)
    return high, (value - high.astype(F32)).astype(BF16)


def dot_nt(a, b):
    return lax.dot_general(a, b, NT, preferred_element_type=F32)


def kernel(
    inv_hbm, pres_ref, fac_hbm, dinv_hbm, off_ref, diag_ref,
    a_raw, a_own, d_raw, f_raw, ft, ft_mate, abuf, asplit, fbuf, ftsplit, pad, q, trecv, vbuf, vrecv,
    ready, load_sem, f_send, f_first, f_near, f_far, x_send, x_recv, a_send, a_recv,
    t_send, t_recv, v_send, v_recv,
):
    r = lax.axis_index("row")
    c = lax.axis_index("col")
    xh = lax.rem(r, 2)
    z = lax.div(r, 2)
    core = lax.rem(c, 2)
    y = lax.rem(lax.div(c, 2), 4)
    xl = lax.div(c, 8)
    chip = lax.div(c, 2)
    r_pair = r + 1 - 2 * xh

    load_a = pltpu.make_async_copy(inv_hbm, a_raw, load_sem.at[0])
    load_f = pltpu.make_async_copy(fac_hbm, f_raw, load_sem.at[1])
    load_d = pltpu.make_async_copy(dinv_hbm, d_raw, load_sem.at[2])

    def send(src, dst, send_sem, recv_sem, peer):
        pltpu.make_async_remote_copy(
            src_ref=src, dst_ref=dst, send_sem=send_sem, recv_sem=recv_sem,
            device_id=peer, device_id_type=MESH,
        ).start()

    def wait(ref, sem):
        pltpu.make_async_copy(ref, ref, sem).wait()

    halves = (xh, xh, 1 - xh, 1 - xh)
    lows = (xl, 1 - xl, 1 - xl, xl)
    rows = (r, r, r_pair, r_pair)

    def column_at(kind, dy, of_core):
        return lows[kind] * 8 + lax.rem(y + dy + 4, 4) * 2 + of_core

    def slot(kind, dy):
        return (halves[kind] * 2 + lows[kind]) * 4 + lax.rem(y + dy + 4, 4)

    def z_peer(dz):
        return (lax.rem(r + 2 * dz + NROW, NROW), c)

    def block_in():
        load_a.wait()
        for b in range(2):
            a_own[b] = a_raw[pl.ds(b, 128, stride=2), :] * pres_ref[0, b].astype(F32)

    def give(kind, dy, b, own):
        send(
            a_own.at[b], abuf.at[own, b], a_send, a_recv.at[kind, (4 - dy) % 4, b],
            (rows[kind], column_at(kind, dy, 0)),
        )

    def give_same_half(own):
        for b in range(2):
            for kind, dy in ((1, 1 - 2 * b), (0, 1 - 2 * b), (1, 0), (0, 2 * b - 1)):
                give(kind, dy, b, own)

    def give_other_half(own):
        for b in range(2):
            for dy in (1, -1):
                give(2, dy, b, own)
        for b in range(2):
            give(2, 0, b, own)

    barrier = pltpu.get_barrier_semaphore()

    def greet(peer):
        pl.semaphore_signal(barrier, inc=1, device_id=peer, device_id_type=MESH)

    def put_update():
        for h in range(4):
            off_ref[:, 128 * h : 128 * (h + 1)] = -(
                vrecv[2 * h] + vrecv[2 * h + 1] + (vrecv[2 * h + 8] + vrecv[2 * h + 9])
            )

    def put_diag():
        tile = trecv[0]
        for step in range(1, NROW):
            tile = tile + trecv[step]
        for g in range(4):
            spots = pl.ds(g, 4, stride=4)
            diag_ref[spots, :] = d_raw[spots, :] + tile[:, 32 * g : 32 * (g + 1)]

    @pl.when(core == 1)
    def _():
        load_a.start()
        load_d.start()
        greet((r_pair, c))
        pl.semaphore_wait(barrier, 11)
        pl.semaphore_signal(ready, inc=1, device_id=(r, c - 1), device_id_type=MESH)
        block_in()
        own = slot(0, 0)

        @pl.when(xh == 1)
        def _():
            give_same_half(own)
            for b in range(2):
                give(0, 0, b, own)

        @pl.when(xh == 0)
        def _():
            give_other_half(own)

        load_d.wait()
        wait(vrecv, v_recv)
        put_update()
        wait(trecv, t_recv)
        put_diag()
        wait(abuf.at[pl.ds(0, 3)], a_send)

        @pl.when(xh == 1)
        def _():
            wait(abuf.at[pl.ds(0, 2)], a_send)

    @pl.when(core == 0)
    def _():
        load_a.start()
        load_f.start()
        load_d.start()
        for kind in range(3):
            for dy in (1, -1, 0):
                greet((rows[kind], column_at(kind, dy, 1)))
        greet((r_pair, c + 1))
        for dz in range(1, JUMP + 1):
            greet(z_peer(dz))
            greet(z_peer(-dz))

        block_in()
        own = slot(0, 0)
        pl.semaphore_wait(ready, 1)

        @pl.when(xh == 0)
        def _():
            give_same_half(own)
            abuf[own] = a_own[...]

        @pl.when(xh == 1)
        def _():
            give_other_half(own)

        load_f.wait()
        for part in range(4):
            ft[128 * part : 128 * (part + 1), :] = f_raw[:, 128 * part : 128 * (part + 1)].T
        own_rows = pl.ds(pl.multiple_of(32 * c, 64), 64)
        fbuf[z] = ft[own_rows, :]
        pl.semaphore_wait(barrier, 2 * JUMP)

        for way, dz in enumerate((JUMP, -JUMP)):
            send(ft.at[own_rows, :], fbuf.at[z], f_send, f_first.at[way], z_peer(dz))
        for dz in (4, -4, 3, -3, 2, -2, 1, -1):
            send(ft.at[own_rows, :], fbuf.at[z], f_send, f_near, z_peer(dz))

        def lay_factor(source, at):
            for g in range(4):
                high, low = split(source[pl.ds(g, 128, stride=4), :])
                ftsplit[0:128, 128 * (4 * at + g) : 128 * (4 * at + g + 1)] = high
                ftsplit[128:256, 128 * (4 * at + g) : 128 * (4 * at + g + 1)] = low

        lay_factor(ft, 0)
        load_d.wait()
        pad[...] = jnp.zeros_like(pad)

        def got(kind, dy, b):
            wait(abuf.at[slot(kind, dy), b], a_recv.at[kind, dy % 4, b])

        def pass_y(kind, dy, b, to):
            at = slot(kind, dy)
            send(
                abuf.at[at, b], abuf.at[at, b], a_send, a_recv.at[kind, (dy - to) % 4, b],
                (r, column_at(0, to, 0)),
            )

        def pass_across(dy, b):
            at = slot(2, dy)
            send(abuf.at[at, b], abuf.at[at, b], a_send, a_recv.at[3, dy % 4, b], (r, column_at(1, 0, 0)))

        for b in range(2):
            got(1, 0, b)
            pass_y(1, 0, b, 2 * b - 1)
            for dy in (-1, 1):
                got(2, dy, b)
                pass_across(dy, b)
                if dy == 2 * b - 1:
                    pass_y(2, dy, b, -dy)
            got(0, 2 * b - 1, b)
            pass_y(0, 2 * b - 1, b, 1 - 2 * b)
        for b in range(2):
            got(2, 0, b)
            pass_across(0, b)
        for b in range(2):
            got(1, 2 * b - 1, b)
            pass_y(1, 2 * b - 1, b, 1 - 2 * b)

        for way in range(2):
            sign = 1 - 2 * way
            at = lax.rem(z - sign * JUMP + 16, 16)
            wait(fbuf.at[at], f_first.at[way])
            half = fbuf.at[at, pl.ds(32 * way, 32)]
            send(half, half, f_send, f_far, z_peer(3 * sign))
            for dz in (2 * sign, sign):
                send(fbuf.at[at], fbuf.at[at], f_send, f_far, z_peer(dz))

        send(ft, ft_mate, x_send, x_recv, (r_pair, column_at(2, 0, 0)))

        for b in range(2):
            got(3, 2 * b - 1, b)
            pass_y(3, 2 * b - 1, b, 1 - 2 * b)

        @pl.when(xh == 1)
        def _():
            for b in range(2):
                got(0, 0, b)

        def lay_piece(kind, dy, b):
            high, low = split(abuf[slot(kind, dy), b])
            at = (lows[kind] * 4 + lax.rem(y + dy + 4, 4)) * 2 + b
            left = 256 * (kind // 2)
            asplit[at, left : left + 128] = high
            asplit[at, left + 128 : left + 256] = low

        def product(low_x, dy, b):
            chip_at = low_x * 4 + lax.rem(y + dy + 4, 4)
            lhs = jnp.concatenate(split(fbuf[chip_at + 8 * b]), axis=0)
            return dot_nt(lhs, asplit[chip_at * 2 + b])

        for b in range(2):
            for kind in (0, 1, 3):
                got(kind, 1 - 2 * b, b)
            got(3, 0, b)
        for kind in range(4):
            for dy in (0, 1, -1):
                for b in range(2):
                    lay_piece(kind, dy, b)
        wait(ft_mate, x_recv)
        lay_factor(ft_mate, 1)
        wait(fbuf.at[pl.ds(0, 8)], f_near)
        wait(fbuf.at[pl.ds(0, 5)], f_far)
        total = jnp.zeros((128, 512), F32)
        for low_x in (xl, 1 - xl):
            for dy in (0, 1, -1):
                for b in range(2):
                    total = total + product(low_x, dy, b)
        for kind in range(4):
            for b in range(2):
                got(kind, 2, b)
                lay_piece(kind, 2, b)
        for low_x in (xl, 1 - xl):
            for b in range(2):
                total = total + product(low_x, 2, b)
        parts = [
            total[:64, 256 * at : 256 * at + 128]
            + (total[:64, 256 * at + 128 : 256 * at + 256] + total[64:, 256 * at : 256 * at + 128])
            for at in range(2)
        ]

        stacks = []
        for part in parts:
            pieces = split(part)
            for g in range(4):
                stack = []
                for of_core in range(2):
                    for piece in pieces:
                        for lane in range(4):
                            here = piece[32 * of_core : 32 * of_core + 32]
                            stack.append(here if lane == g else jnp.zeros((32, 128), BF16))
                stacks.append(jnp.concatenate(stack, axis=0))
        full = dot_nt(ftsplit[...], jnp.concatenate(stacks, axis=1))
        for of_core in range(2):
            left = 256 * of_core
            tiles = full[:128, left : left + 128] + (full[:128, left + 128 : left + 256] + full[128:, left : left + 128])
            q[:, of_core] = tiles.reshape(NROW, 4, 128)
        for at in range(NROW - 1):
            goal = at + (r <= at).astype(jnp.int32)
            step = lax.rem(goal - r + NROW, NROW)
            for of_core in (1, 0):
                send(q.at[goal, of_core], trecv.at[step], t_send, t_recv, (goal, c + of_core))
        send(q.at[r, 1], trecv.at[0], t_send, t_recv, (r, c + 1))
        trecv[0] = q[r, 0]

        half_rows = pl.ds(pl.multiple_of(64 * lax.rem(chip, 2), 64), 64)
        mine = xh * 8 + chip
        for which in range(2):
            pad[which, half_rows, :] = parts[which]
            vbuf[which] = pad[which].T
        vrecv[mine] = vbuf[0, pl.ds(pl.multiple_of(8 * c, 8), 8), :]
        for kind in (3, 2, 1, 0):
            for dy in (2, 3, 1, 0):
                for of_core in range(2):
                    if (kind, dy, of_core) != (0, 0, 0):
                        col = column_at(kind, dy, of_core)
                        slab = vbuf.at[kind // 2, pl.ds(pl.multiple_of(8 * col, 8), 8), :]
                        send(slab, vrecv.at[mine], v_send, v_recv, (rows[kind], col))

        wait(vrecv.at[pl.ds(0, 15)], v_recv)
        put_update()

        wait(trecv.at[pl.ds(1, 31)], t_recv)
        put_diag()

        wait(fbuf.at[pl.ds(0, 15)], f_send)
        wait(ft, x_send)
        wait(abuf.at[pl.ds(0, 11)], a_send)

        @pl.when(xh == 0)
        def _():
            wait(abuf.at[0], a_send)

        wait(q.at[pl.ds(0, 31)], t_send)
        wait(trecv.at[0], t_send)
        wait(vrecv.at[pl.ds(0, 16)], v_send)
        wait(vrecv.at[pl.ds(0, 15)], v_send)


def local(inverse_set, presence, factor, dinv):
    update, diag = pl.pallas_call(
        kernel,
        out_shape=(pltpu.VMEM((8, 512), F32), pltpu.VMEM((16, 32), F32)),
        in_specs=[
            pl.BlockSpec(memory_space=pl.ANY),
            pl.BlockSpec(memory_space=pltpu.SMEM),
            pl.BlockSpec(memory_space=pl.ANY),
            pl.BlockSpec(memory_space=pl.ANY),
        ],
        out_specs=(pl.BlockSpec(memory_space=pltpu.VMEM), pl.BlockSpec(memory_space=pltpu.VMEM)),
        scratch_shapes=[
            pltpu.VMEM((256, 128), F32),
            pltpu.VMEM((2, 128, 128), F32),
            pltpu.VMEM((16, 32), F32),
            pltpu.VMEM((128, 512), F32),
            pltpu.VMEM((512, 128), F32),
            pltpu.VMEM((512, 128), F32),
            pltpu.VMEM((16, 2, 128, 128), F32),
            pltpu.VMEM((16, 512, 128), BF16),
            pltpu.VMEM((16, 64, 128), F32),
            pltpu.VMEM((256, 1024), BF16),
            pltpu.VMEM((2, 128, 128), F32),
            pltpu.VMEM((NROW, 2, 4, 128), F32),
            pltpu.VMEM((NROW, 4, 128), F32),
            pltpu.VMEM((2, 128, 128), F32),
            pltpu.VMEM((16, 8, 128), F32),
            pltpu.SemaphoreType.REGULAR,
            pltpu.SemaphoreType.DMA((3,)),
            pltpu.SemaphoreType.DMA,
            pltpu.SemaphoreType.DMA((2,)),
            pltpu.SemaphoreType.DMA,
            pltpu.SemaphoreType.DMA,
            pltpu.SemaphoreType.DMA,
            pltpu.SemaphoreType.DMA,
            pltpu.SemaphoreType.DMA,
            pltpu.SemaphoreType.DMA((4, 4, 2)),
            pltpu.SemaphoreType.DMA,
            pltpu.SemaphoreType.DMA,
            pltpu.SemaphoreType.DMA,
            pltpu.SemaphoreType.DMA,
        ],
        compiler_params=pltpu.CompilerParams(collective_id=0, has_side_effects=True),
    )(
        inverse_set.reshape(256, 128),
        presence.reshape(1, 2),
        factor.reshape(128, 512),
        dinv,
    )
    return update.reshape(1, 1, 8, 512), diag


def solution(mesh):
    in_specs = (
        P(None, "row", None, None, "col", None),
        P(None, "row", None, "col"),
        P(None, "row", None, None),
        P("row", "col"),
    )
    out_specs = (P(None, "row", "col", None), P("row", "col"))
    return jax.shard_map(local, mesh=mesh, in_specs=in_specs, out_specs=out_specs, check_vma=False)
```

```python
import jax
import jax.numpy as jnp
from jax import lax
from jax.experimental import pallas as pl
from jax.experimental.pallas import tpu as pltpu
from jax.sharding import PartitionSpec as P

MESH = pl.DeviceIdType.MESH
NROW = 32
F32 = jnp.float32
BF16 = jnp.bfloat16
NT = (((1,), (1,)), ((), ()))
JUMP = 5


def split(value):
    high = value.astype(BF16)
    return high, (value - high.astype(F32)).astype(BF16)


def dot_nt(a, b):
    return lax.dot_general(a, b, NT, preferred_element_type=F32)


def kernel(
    inv_hbm, pres_ref, fac_hbm, dinv_hbm, off_ref, diag_ref,
    a_raw, a_own, d_raw, f_raw, ft, ft_mate, abuf, asplit, fbuf, ftsplit, pad, q, trecv, vbuf, vrecv,
    ready, load_sem, f_send, f_first, f_near, f_far, x_send, x_recv, a_send, a_recv,
    t_send, t_recv, v_send, v_recv,
):
    r = lax.axis_index("row")
    c = lax.axis_index("col")
    xh = lax.rem(r, 2)
    z = lax.div(r, 2)
    core = lax.rem(c, 2)
    y = lax.rem(lax.div(c, 2), 4)
    xl = lax.div(c, 8)
    chip = lax.div(c, 2)
    r_pair = r + 1 - 2 * xh

    load_a = pltpu.make_async_copy(inv_hbm, a_raw, load_sem.at[0])
    load_f = pltpu.make_async_copy(fac_hbm, f_raw, load_sem.at[1])
    load_d = pltpu.make_async_copy(dinv_hbm, d_raw, load_sem.at[2])

    def send(src, dst, send_sem, recv_sem, peer):
        pltpu.make_async_remote_copy(
            src_ref=src, dst_ref=dst, send_sem=send_sem, recv_sem=recv_sem,
            device_id=peer, device_id_type=MESH,
        ).start()

    def wait(ref, sem):
        pltpu.make_async_copy(ref, ref, sem).wait()

    halves = (xh, xh, 1 - xh, 1 - xh)
    lows = (xl, 1 - xl, 1 - xl, xl)
    rows = (r, r, r_pair, r_pair)

    def column_at(kind, dy, of_core):
        return lows[kind] * 8 + lax.rem(y + dy + 4, 4) * 2 + of_core

    def slot(kind, dy):
        return (halves[kind] * 2 + lows[kind]) * 4 + lax.rem(y + dy + 4, 4)

    def z_peer(dz):
        return (lax.rem(r + 2 * dz + NROW, NROW), c)

    def block_in():
        load_a.wait()
        for b in range(2):
            a_own[b] = a_raw[pl.ds(b, 128, stride=2), :] * pres_ref[0, b].astype(F32)

    def give(kind, dy, b, own):
        send(
            a_own.at[b], abuf.at[own, b], a_send, a_recv.at[kind, (4 - dy) % 4, b],
            (rows[kind], column_at(kind, dy, 0)),
        )

    def give_same_half(own):
        for b in range(2):
            for kind, dy in ((1, 1 - 2 * b), (0, 1 - 2 * b), (1, 0), (0, 2 * b - 1)):
                give(kind, dy, b, own)

    def give_other_half(own):
        for b in range(2):
            for dy in (1, -1):
                give(2, dy, b, own)
        for b in range(2):
            give(2, 0, b, own)

    barrier = pltpu.get_barrier_semaphore()

    def greet(peer):
        pl.semaphore_signal(barrier, inc=1, device_id=peer, device_id_type=MESH)

    def put_update():
        for h in range(4):
            off_ref[:, 128 * h : 128 * (h + 1)] = -(
                vrecv[2 * h] + vrecv[2 * h + 1] + (vrecv[2 * h + 8] + vrecv[2 * h + 9])
            )

    def put_diag():
        tile = trecv[0]
        for step in range(1, NROW):
            tile = tile + trecv[step]
        for g in range(4):
            spots = pl.ds(g, 4, stride=4)
            diag_ref[spots, :] = d_raw[spots, :] + tile[:, 32 * g : 32 * (g + 1)]

    @pl.when(core == 1)
    def _():
        load_a.start()
        load_d.start()
        greet((r_pair, c))
        pl.semaphore_wait(barrier, 11)
        pl.semaphore_signal(ready, inc=1, device_id=(r, c - 1), device_id_type=MESH)
        block_in()
        own = slot(0, 0)

        @pl.when(xh == 1)
        def _():
            give_same_half(own)
            for b in range(2):
                give(0, 0, b, own)

        @pl.when(xh == 0)
        def _():
            give_other_half(own)

        load_d.wait()
        wait(vrecv, v_recv)
        put_update()
        wait(trecv, t_recv)
        put_diag()
        wait(abuf.at[pl.ds(0, 3)], a_send)

        @pl.when(xh == 1)
        def _():
            wait(abuf.at[pl.ds(0, 2)], a_send)

    @pl.when(core == 0)
    def _():
        load_a.start()
        load_f.start()
        load_d.start()
        for kind in range(3):
            for dy in (1, -1, 0):
                greet((rows[kind], column_at(kind, dy, 1)))
        greet((r_pair, c + 1))
        for dz in range(1, JUMP + 1):
            greet(z_peer(dz))
            greet(z_peer(-dz))

        block_in()
        own = slot(0, 0)
        pl.semaphore_wait(ready, 1)

        @pl.when(xh == 0)
        def _():
            give_same_half(own)
            abuf[own] = a_own[...]

        @pl.when(xh == 1)
        def _():
            give_other_half(own)

        load_f.wait()
        for part in range(4):
            ft[128 * part : 128 * (part + 1), :] = f_raw[:, 128 * part : 128 * (part + 1)].T
        own_rows = pl.ds(pl.multiple_of(32 * c, 64), 64)
        fbuf[z] = ft[own_rows, :]
        pl.semaphore_wait(barrier, 2 * JUMP)

        for way, dz in enumerate((JUMP, -JUMP)):
            send(ft.at[own_rows, :], fbuf.at[z], f_send, f_first.at[way], z_peer(dz))
        for dz in (4, -4, 3, -3, 2, -2, 1, -1):
            send(ft.at[own_rows, :], fbuf.at[z], f_send, f_near, z_peer(dz))

        def lay_factor(source, at):
            for g in range(4):
                high, low = split(source[pl.ds(g, 128, stride=4), :])
                ftsplit[0:128, 128 * (4 * at + g) : 128 * (4 * at + g + 1)] = high
                ftsplit[128:256, 128 * (4 * at + g) : 128 * (4 * at + g + 1)] = low

        lay_factor(ft, 0)
        load_d.wait()
        pad[...] = jnp.zeros_like(pad)

        def got(kind, dy, b):
            wait(abuf.at[slot(kind, dy), b], a_recv.at[kind, dy % 4, b])

        def pass_y(kind, dy, b, to):
            at = slot(kind, dy)
            send(
                abuf.at[at, b], abuf.at[at, b], a_send, a_recv.at[kind, (dy - to) % 4, b],
                (r, column_at(0, to, 0)),
            )

        def pass_across(dy, b):
            at = slot(2, dy)
            send(abuf.at[at, b], abuf.at[at, b], a_send, a_recv.at[3, dy % 4, b], (r, column_at(1, 0, 0)))

        for b in range(2):
            got(1, 0, b)
            pass_y(1, 0, b, 2 * b - 1)
            got(1, 2 * b - 1, b)
            pass_y(1, 2 * b - 1, b, 1 - 2 * b)
            for dy in (-1, 1):
                got(2, dy, b)
                pass_across(dy, b)
                if dy == 2 * b - 1:
                    pass_y(2, dy, b, -dy)
            got(0, 2 * b - 1, b)
            pass_y(0, 2 * b - 1, b, 1 - 2 * b)
        for b in range(2):
            got(2, 0, b)
            pass_across(0, b)

        for way in range(2):
            sign = 1 - 2 * way
            at = lax.rem(z - sign * JUMP + 16, 16)
            wait(fbuf.at[at], f_first.at[way])
            half = fbuf.at[at, pl.ds(32 * way, 32)]
            send(half, half, f_send, f_far, z_peer(3 * sign))
            for dz in (2 * sign, sign):
                send(fbuf.at[at], fbuf.at[at], f_send, f_far, z_peer(dz))

        send(ft, ft_mate, x_send, x_recv, (r_pair, column_at(2, 0, 0)))

        for b in range(2):
            got(3, 2 * b - 1, b)
            pass_y(3, 2 * b - 1, b, 1 - 2 * b)

        @pl.when(xh == 1)
        def _():
            for b in range(2):
                got(0, 0, b)

        def lay_piece(kind, dy, b):
            high, low = split(abuf[slot(kind, dy), b])
            at = (lows[kind] * 4 + lax.rem(y + dy + 4, 4)) * 2 + b
            left = 256 * (kind // 2)
            asplit[at, left : left + 128] = high
            asplit[at, left + 128 : left + 256] = low

        def product(low_x, dy, b):
            chip_at = low_x * 4 + lax.rem(y + dy + 4, 4)
            lhs = jnp.concatenate(split(fbuf[chip_at + 8 * b]), axis=0)
            return dot_nt(lhs, asplit[chip_at * 2 + b])

        for b in range(2):
            for kind in (0, 1, 3):
                got(kind, 1 - 2 * b, b)
            got(3, 0, b)
        for kind in range(4):
            for dy in (0, 1, -1):
                for b in range(2):
                    lay_piece(kind, dy, b)
        wait(ft_mate, x_recv)
        lay_factor(ft_mate, 1)
        wait(fbuf.at[pl.ds(0, 8)], f_near)
        wait(fbuf.at[pl.ds(0, 5)], f_far)
        total = jnp.zeros((128, 512), F32)
        for low_x in (xl, 1 - xl):
            for dy in (0, 1, -1):
                for b in range(2):
                    total = total + product(low_x, dy, b)
        for kind in range(4):
            for b in range(2):
                got(kind, 2, b)
                lay_piece(kind, 2, b)
        for low_x in (xl, 1 - xl):
            for b in range(2):
                total = total + product(low_x, 2, b)
        parts = [
            total[:64, 256 * at : 256 * at + 128]
            + (total[:64, 256 * at + 128 : 256 * at + 256] + total[64:, 256 * at : 256 * at + 128])
            for at in range(2)
        ]

        stacks = []
        for part in parts:
            pieces = split(part)
            for g in range(4):
                stack = []
                for of_core in range(2):
                    for piece in pieces:
                        for lane in range(4):
                            here = piece[32 * of_core : 32 * of_core + 32]
                            stack.append(here if lane == g else jnp.zeros((32, 128), BF16))
                stacks.append(jnp.concatenate(stack, axis=0))
        full = dot_nt(ftsplit[...], jnp.concatenate(stacks, axis=1))
        for of_core in range(2):
            left = 256 * of_core
            tiles = full[:128, left : left + 128] + (full[:128, left + 128 : left + 256] + full[128:, left : left + 128])
            q[:, of_core] = tiles.reshape(NROW, 4, 128)
        for at in range(NROW - 1):
            goal = at + (r <= at).astype(jnp.int32)
            step = lax.rem(goal - r + NROW, NROW)
            for of_core in (1, 0):
                send(q.at[goal, of_core], trecv.at[step], t_send, t_recv, (goal, c + of_core))
        send(q.at[r, 1], trecv.at[0], t_send, t_recv, (r, c + 1))
        trecv[0] = q[r, 0]

        half_rows = pl.ds(pl.multiple_of(64 * lax.rem(chip, 2), 64), 64)
        mine = xh * 8 + chip
        for which in range(2):
            pad[which, half_rows, :] = parts[which]
            vbuf[which] = pad[which].T
        vrecv[mine] = vbuf[0, pl.ds(pl.multiple_of(8 * c, 8), 8), :]
        for kind in (3, 2, 1, 0):
            for dy in (2, 3, 1, 0):
                for of_core in range(2):
                    if (kind, dy, of_core) != (0, 0, 0):
                        col = column_at(kind, dy, of_core)
                        slab = vbuf.at[kind // 2, pl.ds(pl.multiple_of(8 * col, 8), 8), :]
                        send(slab, vrecv.at[mine], v_send, v_recv, (rows[kind], col))

        wait(vrecv.at[pl.ds(0, 15)], v_recv)
        put_update()

        wait(trecv.at[pl.ds(1, 31)], t_recv)
        put_diag()

        wait(fbuf.at[pl.ds(0, 15)], f_send)
        wait(ft, x_send)
        wait(abuf.at[pl.ds(0, 11)], a_send)

        @pl.when(xh == 0)
        def _():
            wait(abuf.at[0], a_send)

        wait(q.at[pl.ds(0, 31)], t_send)
        wait(trecv.at[0], t_send)
        wait(vrecv.at[pl.ds(0, 16)], v_send)
        wait(vrecv.at[pl.ds(0, 15)], v_send)


def local(inverse_set, presence, factor, dinv):
    update, diag = pl.pallas_call(
        kernel,
        out_shape=(pltpu.VMEM((8, 512), F32), pltpu.VMEM((16, 32), F32)),
        in_specs=[
            pl.BlockSpec(memory_space=pl.ANY),
            pl.BlockSpec(memory_space=pltpu.SMEM),
            pl.BlockSpec(memory_space=pl.ANY),
            pl.BlockSpec(memory_space=pl.ANY),
        ],
        out_specs=(pl.BlockSpec(memory_space=pltpu.VMEM), pl.BlockSpec(memory_space=pltpu.VMEM)),
        scratch_shapes=[
            pltpu.VMEM((256, 128), F32),
            pltpu.VMEM((2, 128, 128), F32),
            pltpu.VMEM((16, 32), F32),
            pltpu.VMEM((128, 512), F32),
            pltpu.VMEM((512, 128), F32),
            pltpu.VMEM((512, 128), F32),
            pltpu.VMEM((16, 2, 128, 128), F32),
            pltpu.VMEM((16, 512, 128), BF16),
            pltpu.VMEM((16, 64, 128), F32),
            pltpu.VMEM((256, 1024), BF16),
            pltpu.VMEM((2, 128, 128), F32),
            pltpu.VMEM((NROW, 2, 4, 128), F32),
            pltpu.VMEM((NROW, 4, 128), F32),
            pltpu.VMEM((2, 128, 128), F32),
            pltpu.VMEM((16, 8, 128), F32),
            pltpu.SemaphoreType.REGULAR,
            pltpu.SemaphoreType.DMA((3,)),
            pltpu.SemaphoreType.DMA,
            pltpu.SemaphoreType.DMA((2,)),
            pltpu.SemaphoreType.DMA,
            pltpu.SemaphoreType.DMA,
            pltpu.SemaphoreType.DMA,
            pltpu.SemaphoreType.DMA,
            pltpu.SemaphoreType.DMA,
            pltpu.SemaphoreType.DMA((4, 4, 2)),
            pltpu.SemaphoreType.DMA,
            pltpu.SemaphoreType.DMA,
            pltpu.SemaphoreType.DMA,
            pltpu.SemaphoreType.DMA,
        ],
        compiler_params=pltpu.CompilerParams(collective_id=0, has_side_effects=True),
    )(
        inverse_set.reshape(256, 128),
        presence.reshape(1, 2),
        factor.reshape(128, 512),
        dinv,
    )
    return update.reshape(1, 1, 8, 512), diag


def solution(mesh):
    in_specs = (
        P(None, "row", None, None, "col", None),
        P(None, "row", None, "col"),
        P(None, "row", None, None),
        P("row", "col"),
    )
    out_specs = (P(None, "row", "col", None), P("row", "col"))
    return jax.shard_map(local, mesh=mesh, in_specs=in_specs, out_specs=out_specs, check_vma=False)
```
